32 devices in a mesh: dp: 2 (over y), space: 4 (over z), chan: 4 (over x, core).
Axes of the slice: x: 2, y: 2, z: 4, core: 2. Of those that a mesh axis runs over, the one named last changes fastest.
Arguments:
- volumes: bfloat16 [2, 8, 512, 1024], P('dp', 'space', 'chan'), may hold values from -6 to 6
- kernel: bfloat16 [512, 13824], P('chan'), may hold values from -0.15625 to 0.15625
- bias: float32 [512], P('chan'), may hold values from -3 to 3
- act_grad: bfloat16 [2, 4, 512, 256], P('dp', 'space', 'chan'), may hold values from -6 to 6
Outputs:
- activation: bfloat16 [2, 4, 512, 256], P('dp', 'space', 'chan')
- grad_x: bfloat16 [2, 8, 512, 1024], P('dp', 'space', 'chan')
- grad_w: float32 [512, 13824], P('chan')
- grad_b: float32 [512], P('chan')
The draws below stay inside these ranges and needn't reach their ends.
All inputs are finite; a program needn't handle non-finite values.
Results may differ from the reference program's by a relative error of at most 0.005.
Values may be sent and summed in bfloat16 or wider, within the bound.
A program may use at most 64 MiB of HBM per device.

```python
import jax
import jax.numpy as jnp
from jax import lax

CIN = 512
COUT = 512
GRID = 32
VOLUMES = 2
GX = 8
OX = 4
OG = 16
N_CHAN = 4


def shard_levels(key, shape, split, low, top_value):
    factor_of = 1.0
    for position, blocks in split:
        draws = jax.random.uniform(jax.random.fold_in(jax.random.fold_in(key, 6), position), (blocks,), jnp.float32, low / len(split), top_value / len(split))
        factor_of = factor_of * jnp.repeat(jnp.exp(draws), shape[position] // blocks).reshape((-1,) + (1,) * (len(shape) - 1 - position))
    return factor_of


def noise(own_key, extent, scale, most, split=(), held_as=jnp.bfloat16):
    array = scale * jax.random.normal(own_key, extent, jnp.float32)
    if split:
        array = array * shard_levels(own_key, extent, split, -0.22, 0.18)
    return jnp.clip(array, -most, most).astype(held_as)


def setup_inputs(seed: int = 0) -> dict:
    seeds = jax.random.split(jax.random.key(seed), 5)
    volumes = noise(seeds[0], (VOLUMES, GX, CIN, GRID * GRID), 1.0, 6.0, ((0, 2), (1, 4), (2, 4)))
    kernel = noise(seeds[1], (COUT, 27 * CIN), (27 * CIN // 8) ** -0.5, 0.15625, ((0, 4),))
    bias = noise(seeds[2], (COUT,), 0.5, 3.0, ((0, 4),), jnp.float32)
    act_grad = noise(seeds[3], (VOLUMES, OX, COUT, OG * OG), 1.0, 6.0, ((0, 2), (1, 4), (2, 4)))
    return dict(volumes=volumes, kernel=kernel, bias=bias, act_grad=act_grad)


NUMBERS = ('NDHWC', 'DHWIO', 'NDHWC')

def forward_conv(inputs, filters):
    return lax.conv_general_dilated(inputs, filters, (2, 2, 2), ((1, 1), (1, 1), (1, 1)), dimension_numbers=NUMBERS, preferred_element_type=jnp.float32)

def transpose_conv(grads, flipped):
    return lax.conv_general_dilated(grads, flipped, (1, 1, 1), ((1, 2), (1, 2), (1, 2)), lhs_dilation=(2, 2, 2), dimension_numbers=NUMBERS, preferred_element_type=jnp.float32)

def reference(volumes, kernel, bias, act_grad):
    total_vols = volumes.shape[0]
    vol_cells = volumes.reshape(total_vols, GX, CIN, GRID, GRID).transpose(0, 1, 3, 4, 2)
    filters = kernel.reshape(COUT, 3, 3, 3, CIN).transpose(1, 2, 3, 4, 0)
    grad_cells = act_grad.reshape(total_vols, OX, COUT, OG, OG).transpose(0, 1, 3, 4, 2)
    pre_act = forward_conv(vol_cells, filters) + bias
    activation = jax.nn.gelu(pre_act).astype(jnp.bfloat16)
    _, pull_back = jax.vjp(jax.nn.gelu, pre_act)
    out_grad = pull_back(grad_cells.astype(jnp.float32))[0].astype(jnp.bfloat16)
    group_width = COUT // N_CHAN
    flipped = filters[::-1, ::-1, ::-1].transpose(0, 1, 2, 4, 3)
    total = jnp.zeros(vol_cells.shape, jnp.float32)
    for group in range(N_CHAN):
        lower = group * group_width
        partial_grad = transpose_conv(out_grad[..., lower:lower + group_width], flipped[:, :, :, lower:lower + group_width, :])
        total = total + partial_grad
    grad_cells_x = total.astype(jnp.bfloat16)
    padded = jnp.pad(vol_cells, ((0, 0), (1, 1), (1, 1), (1, 1), (0, 0)))
    out_x, out_y, out_z = (out_grad.shape[1], out_grad.shape[2], out_grad.shape[3])
    flat_grad = out_grad.reshape(-1, COUT)
    tap_terms = []
    for first_tap in range(3):
        for second_tap in range(3):
            for third_tap in range(3):
                window = padded[:, first_tap:first_tap + 2 * out_x:2, second_tap:second_tap + 2 * out_y:2, third_tap:third_tap + 2 * out_z:2, :]
                tap_terms.append(lax.dot_general(window.reshape(-1, CIN), flat_grad, (((0,), (0,)), ((), ())), preferred_element_type=jnp.float32))
    weight_old = jnp.stack(tap_terms).reshape(3, 3, 3, CIN, COUT) / VOLUMES
    grad_b = lax.optimization_barrier(jnp.sum(out_grad.astype(jnp.float32), axis=(0, 1, 2, 3))) / VOLUMES
    activation_out = activation.transpose(0, 1, 4, 2, 3).reshape(total_vols, OX, COUT, OG * OG)
    grad_x = grad_cells_x.transpose(0, 1, 4, 2, 3).reshape(total_vols, GX, CIN, GRID * GRID)
    grad_w = weight_old.transpose(4, 0, 1, 2, 3).reshape(COUT, 27 * CIN)
    return (activation_out, grad_x, grad_w, grad_b)
```

```python
import functools

import jax
import jax.numpy as jnp
from jax import lax
from jax.experimental import pallas as pl
from jax.experimental.pallas import tpu as pltpu
from jax.sharding import PartitionSpec as P

GRID = 32
HALF = GRID // 2
CELLS = HALF * HALF
BF = jnp.bfloat16
F32 = jnp.float32
VM = pl.BlockSpec(memory_space=pltpu.VMEM)
TAPS = [(k1, k2, k3) for k1 in range(3) for k2 in range(3) for k3 in range(3)]


def phase_of(k2, k3):
    return 2 * (k2 != 1) + (k3 != 1)


def shift_of(k2, k3):
    return 2 * (k2 == 0) + (k3 == 0)


def parity_matrix():
    full = GRID * GRID
    dst = lax.broadcasted_iota(jnp.int32, (1, full), 1)
    phase, cell = dst // CELLS, dst % CELLS
    y = 2 * (cell // HALF) + phase // 2
    z = 2 * (cell % HALF) + phase % 2
    src = y * GRID + z
    rows = lax.broadcasted_iota(jnp.int32, (full, full), 0)
    return jnp.where(rows == src, 1.0, 0.0).astype(BF)


def lanes():
    return lax.broadcasted_iota(jnp.int32, (1, CELLS), 1)


def forward_shift(x, s):
    if s & 2:
        x = jnp.where(lanes() >= HALF, pltpu.roll(x, HALF, 1), 0.0)
    if s & 1:
        x = jnp.where(lanes() % HALF != 0, pltpu.roll(x, 1, 1), 0.0)
    return x


def backward_shift(x, s):
    if s & 2:
        x = jnp.where(lanes() < CELLS - HALF, pltpu.roll(x, CELLS - HALF, 1), 0.0)
    if s & 1:
        x = jnp.where(lanes() % HALF != HALF - 1, pltpu.roll(x, CELLS - 1, 1), 0.0)
    return x


def split_kernel(v_ref, p_ref, o_ref):
    o_ref[...] = jnp.dot(v_ref[...], p_ref[...], preferred_element_type=F32).astype(BF)


def merge_kernel(v_ref, p_ref, o_ref):
    total = v_ref[0].astype(F32)
    for j in range(1, v_ref.shape[0]):
        total = total + v_ref[j].astype(F32)
    o_ref[...] = lax.dot_general(
        total.astype(BF).reshape(o_ref.shape), p_ref[...], (((1,), (1,)), ((), ())), preferred_element_type=F32
    ).astype(BF)


def send(src, dst, send_sem, recv_sem, device):
    return pltpu.make_async_remote_copy(
        src, dst, send_sem, recv_sem, device_id=device, device_id_type=pl.DeviceIdType.MESH
    )


def place():
    return lax.axis_index("dp"), lax.axis_index("space"), lax.axis_index("chan")


def greet(sizes):
    n_dp, n_space, n_chan = sizes
    y, z, c = place()
    barrier = pltpu.get_barrier_semaphore()
    g = y * n_space + z
    for o in range(1, n_chan):
        pl.semaphore_signal(
            barrier, 1, device_id=(y, z, (c + o) % n_chan), device_id_type=pl.DeviceIdType.MESH
        )
    for o in range(1, n_dp * n_space):
        h = (g + o) % (n_dp * n_space)
        pl.semaphore_signal(
            barrier, 1, device_id=(h // n_space, h % n_space, c), device_id_type=pl.DeviceIdType.MESH
        )
    pl.semaphore_wait(barrier, n_chan + n_dp * n_space - 2)


def gather_inputs(sizes, own_ref, x_ref, out_sem, in_sem, local_sem):
    n_dp, n_space, n_chan = sizes
    chips = n_chan // 2
    y, z, c = place()
    chip, core = c // 2, c % 2
    twin = (y, z, 2 * chip + 1 - core)
    greet(sizes)

    def planes(k):
        return pl.ds(1, 2) if k else pl.ds(0, 1)

    def block(k, j):
        return x_ref.at[planes(k), j]

    def to_chip(k, o, src):
        return send(
            src, block(k, c), out_sem.at[k, 0, o], in_sem.at[k, c],
            (y, z, 2 * ((chip + o) % chips) + core),
        )

    def to_twin(k, o, src):
        j = 2 * ((chip - o + chips) % chips) + core
        return send(src, block(k, j), out_sem.at[k, 1, o], in_sem.at[k, j], twin)

    def arrived(k, j):
        send(block(k, j), block(k, j), out_sem.at[k, 1, 0], in_sem.at[k, j], twin).wait_recv()

    rim = send(own_ref.at[pl.ds(1, 1)], block(0, c), out_sem.at[0, 2, 0], in_sem.at[0, c], (y, jnp.minimum(z + 1, n_space - 1), c))
    sends = [to_chip(1, o, own_ref) for o in range(1, chips)] + [to_twin(1, 0, own_ref)]

    @pl.when(z < n_space - 1)
    def _():
        rim.start()

    for copy in sends:
        copy.start()
    keep = pltpu.make_async_copy(own_ref, block(1, c), local_sem)
    keep.start()

    rim_out = [to_chip(0, o, block(0, c)) for o in range(1, chips)] + [to_twin(0, 0, block(0, c))]

    @pl.when(z > 0)
    def _():
        arrived(0, c)
        for copy in rim_out:
            copy.start()

    @pl.when(z == 0)
    def _():
        x_ref[0] = jnp.zeros_like(x_ref[0])

    for o in range(1, chips):
        j = 2 * ((chip - o + chips) % chips) + core
        arrived(1, j)
        passed = to_twin(1, o, block(1, j))
        passed.start()
        sends.append(passed)

    @pl.when(z > 0)
    def _():
        for o in range(1, chips):
            j = 2 * ((chip - o + chips) % chips) + core
            arrived(0, j)
            passed = to_twin(0, o, block(0, j))
            passed.start()
            rim_out.append(passed)
        for o in range(chips):
            arrived(0, 2 * ((chip - o + chips) % chips) + 1 - core)
        for copy in rim_out:
            copy.wait_send()

    for o in range(chips):
        arrived(1, 2 * ((chip - o + chips) % chips) + 1 - core)
    for copy in sends:
        copy.wait_send()

    @pl.when(z < n_space - 1)
    def _():
        rim.wait_send()

    keep.wait()


def forward_kernel(
    sizes, width, own_ref, w_ref, b_ref, g_ref, x_ref, act_ref, dy_ref, db_ref, out_sem, in_sem, local_sem
):
    gather_inputs(sizes, own_ref, x_ref, out_sem, in_sem, local_sem)
    sums = [None] * 4
    for t, (k1, k2, k3) in enumerate(TAPS):
        ph, s = phase_of(k2, k3), shift_of(k2, k3)
        part = jnp.dot(
            w_ref[:, t * width : (t + 1) * width],
            x_ref[k1, :, :, ph * CELLS : (ph + 1) * CELLS].reshape(width, CELLS),
            preferred_element_type=F32,
        )
        sums[s] = part if sums[s] is None else sums[s] + part
    u = b_ref[...] + sums[0]
    for s in (1, 2, 3):
        u = u + forward_shift(sums[s], s)
    c = 0.7978845608028654
    th = jnp.tanh(c * (u + 0.044715 * (u * u * u)))
    act_ref[...] = (0.5 * u * (1.0 + th)).astype(BF)
    slope = 0.5 * (1.0 + th) + 0.5 * u * (1.0 - th * th) * c * (1.0 + 3 * 0.044715 * u * u)
    dy = (g_ref[...].astype(F32) * slope).astype(BF)
    dy_ref[...] = dy
    db_ref[...] = lax.dot_general(
        jnp.ones((8, CELLS), BF), dy, (((1,), (1,)), ((), ())), preferred_element_type=F32
    )


def shifted(dy):
    wide = dy.astype(F32)
    return [dy] + [backward_shift(wide, s).astype(BF) for s in (1, 2, 3)]


def grads_kernel(sizes, width, x_ref, w_ref, dy_ref, dw_ref, gx_ref, next_ref, out_sem, in_sem):
    n_space = sizes[1]
    y, z, c = place()
    greet(sizes)
    back = send(dy_ref, next_ref, out_sem, in_sem, (y, jnp.maximum(z - 1, 0), c))

    @pl.when(z > 0)
    def _():
        back.start()

    own = shifted(dy_ref[...])
    for t, (k1, k2, k3) in enumerate(TAPS):
        ph, s = phase_of(k2, k3), shift_of(k2, k3)
        part = lax.dot_general(
            own[s],
            x_ref[k1, :, :, ph * CELLS : (ph + 1) * CELLS].reshape(width, CELLS),
            (((1,), (1,)), ((), ())),
            preferred_element_type=F32,
        )
        dw_ref[:, t * width : (t + 1) * width] = part.astype(BF)

    @pl.when(z < n_space - 1)
    def _():
        back.wait_recv()

    @pl.when(z == n_space - 1)
    def _():
        next_ref[...] = jnp.zeros_like(next_ref)

    following = shifted(next_ref[...])
    for plane in range(2):
        for ph in range(4):
            total = None
            for t, (k1, k2, k3) in enumerate(TAPS):
                if phase_of(k2, k3) != ph or (k1 == 1) != (plane == 0):
                    continue
                views = following if k1 == 0 else own
                part = lax.dot_general(
                    w_ref[:, t * width : (t + 1) * width],
                    views[shift_of(k2, k3)],
                    (((0,), (0,)), ((), ())),
                    preferred_element_type=F32,
                )
                total = part if total is None else total + part
            gx_ref[:, plane, :, ph * CELLS : (ph + 1) * CELLS] = total.astype(BF).reshape(
                gx_ref.shape[0], gx_ref.shape[2], CELLS
            )

    @pl.when(z > 0)
    def _():
        back.wait_send()


def share_kernel(
    sizes, dw_ref, gx_ref, db_ref, all_ref, parts_ref, dbs_ref, y_ref, r_ref, l_ref, s_ref,
    out_sem, in_sem, gx_out, gx_in, db_out, db_in, local_sem, y_out, y_in, z_out, r_in, l_in
):
    n_dp, n_space, n_chan = sizes
    group = n_dp * n_space
    y, z, c = place()
    g = y * n_space + z
    greet(sizes)
    right = (y, jnp.minimum(z + 1, n_space - 1), c)
    left = (y, jnp.maximum(z - 1, 0), c)
    across = (1 - y, z, c)

    def hop(way, device, j, src=None):
        slot = all_ref.at[y * n_space + j]
        return send(slot if src is None else src, slot, out_sem.at[way, j], in_sem.at[y * n_space + j], device)

    def arrived(h):
        send(all_ref.at[h], all_ref.at[h], out_sem.at[2, 0], in_sem.at[h], across).wait_recv()

    locals_ = [
        pltpu.make_async_copy(gx_ref.at[c], parts_ref.at[c], local_sem.at[1]),
        pltpu.make_async_copy(db_ref, dbs_ref.at[g], local_sem.at[2]),
    ]

    def over(j):
        return send(dw_ref.at[(1 - y) * n_space + j], y_ref.at[j], y_out.at[j], y_in.at[j], across)

    def rightward(j):
        return send(s_ref.at[j], r_ref.at[j], z_out.at[j], r_in.at[j], right)

    def leftward(j):
        return send(s_ref.at[j], l_ref.at[j], z_out.at[j], l_in.at[j], left)

    def both(j):
        over(j).wait_recv()
        return dw_ref[y * n_space + j].astype(F32) + y_ref[j].astype(F32)

    for d in range(n_space - 1, 0, -1):
        @pl.when(z + d < n_space)
        def _():
            over(jnp.minimum(z + d, n_space - 1)).start()

        @pl.when(z - d >= 0)
        def _():
            over(jnp.maximum(z - d, 0)).start()

    over(z).start()
    extra = []
    for o in range(1, n_chan):
        to = (c + o) % n_chan
        extra.append(
            send(gx_ref.at[to], parts_ref.at[c], gx_out.at[o], gx_in.at[o], (y, z, to))
        )
    for o in range(1, group):
        to = (g + o) % group
        extra.append(
            send(db_ref, dbs_ref.at[g], db_out.at[o], db_in.at[o], (to // n_space, to % n_space, c))
        )
    for copy in extra:
        copy.start()
    for copy in locals_:
        copy.start()

    for d in range(n_space - 1, 0, -1):
        @pl.when(z + d < n_space)
        def _():
            j = jnp.minimum(z + d, n_space - 1)
            mine = both(j)

            @pl.when(z == 0)
            def _():
                s_ref[j] = mine.astype(BF)

            @pl.when(z > 0)
            def _():
                rightward(j).wait_recv()
                s_ref[j] = (mine + r_ref[j].astype(F32)).astype(BF)

            rightward(j).start()

        @pl.when(z - d >= 0)
        def _():
            j = jnp.maximum(z - d, 0)
            mine = both(j)

            @pl.when(z == n_space - 1)
            def _():
                s_ref[j] = mine.astype(BF)

            @pl.when(z < n_space - 1)
            def _():
                leftward(j).wait_recv()
                s_ref[j] = (mine + l_ref[j].astype(F32)).astype(BF)

            leftward(j).start()

    @pl.when(z == 0)
    def _():
        r_ref[z] = jnp.zeros_like(r_ref[z])

    @pl.when(z == n_space - 1)
    def _():
        l_ref[z] = jnp.zeros_like(l_ref[z])

    @pl.when(z > 0)
    def _():
        rightward(z).wait_recv()

    @pl.when(z < n_space - 1)
    def _():
        leftward(z).wait_recv()

    all_ref[g] = (both(z) + r_ref[z].astype(F32) + l_ref[z].astype(F32)).astype(BF)

    @pl.when(z < n_space - 1)
    def _():
        hop(0, right, z).start()

    @pl.when(z > 0)
    def _():
        hop(1, left, z).start()

    hop(2, across, z).start()

    for d in range(1, n_space):
        @pl.when(z - d >= 0)
        def _():
            j = jnp.maximum(z - d, 0)
            arrived(y * n_space + j)

            @pl.when(z < n_space - 1)
            def _():
                hop(0, right, j).start()

            hop(2, across, j).start()

        @pl.when(z + d < n_space)
        def _():
            j = jnp.minimum(z + d, n_space - 1)
            arrived(y * n_space + j)

            @pl.when(z > 0)
            def _():
                hop(1, left, j).start()

            hop(2, across, j).start()

    for o in range(1, n_chan):
        frm = (c - o + n_chan) % n_chan
        send(parts_ref.at[frm], parts_ref.at[frm], gx_out.at[o], gx_in.at[o], (y, z, frm)).wait_recv()
    for o in range(1, group):
        frm = (g - o + group) % group
        send(dbs_ref.at[frm], dbs_ref.at[frm], db_out.at[o], db_in.at[o], (frm // n_space, frm % n_space, c)).wait_recv()
    for j in range(n_space):
        arrived((1 - y) * n_space + j)
        hop(2, across, j).wait_send()

        @pl.when((j <= z) & (z < n_space - 1))
        def _():
            hop(0, right, j).wait_send()

        @pl.when((j >= z) & (z > 0))
        def _():
            hop(1, left, j).wait_send()

        over(j).wait_send()

        @pl.when(j > z)
        def _():
            rightward(j).wait_send()

        @pl.when(j < z)
        def _():
            leftward(j).wait_send()

    for copy in extra:
        copy.wait_send()
    for copy in locals_:
        copy.wait()


def call(kernel, out_shape, n_in, flops, moved, scratch=(), collective_id=None):
    many = isinstance(out_shape, (tuple, list))
    return pl.pallas_call(
        kernel,
        out_shape=out_shape,
        in_specs=[VM] * n_in,
        out_specs=[VM] * len(out_shape) if many else VM,
        scratch_shapes=scratch,
        compiler_params=pltpu.CompilerParams(
            vmem_limit_bytes=48 << 20,
            collective_id=collective_id,
            has_side_effects=collective_id is not None,
        ),
        cost_estimate=pl.CostEstimate(flops=flops, bytes_accessed=moved, transcendentals=0),
    )


def shape(*dims, dtype=BF):
    return jax.ShapeDtypeStruct(dims, dtype)


def per_device(volumes, kernel, bias, act_grad):
    batch, planes, part, cells = volumes.shape
    filters = kernel.shape[0]
    width = kernel.shape[1] // 27
    parity = parity_matrix()
    own = call(split_kernel, shape(planes * part, cells), 2, 2 * planes * part * cells**2, 1 << 20)(
        volumes.reshape(planes * part, cells), parity
    ).reshape(planes, part, cells)
    sizes = tuple(lax.axis_size(a) for a in ("dp", "space", "chan"))
    group, n_chan = sizes[0] * sizes[1], sizes[2]
    dma = pltpu.SemaphoreType.DMA
    flops = 2 * 27 * width * filters * CELLS
    x_all, act, dy, db = call(
        functools.partial(forward_kernel, sizes, width),
        (
            shape(3, n_chan, part, cells),
            shape(filters, CELLS),
            shape(filters, CELLS),
            shape(8, filters, dtype=F32),
        ),
        4,
        flops,
        10 << 20,
        scratch=(dma((2, 3, n_chan // 2)), dma((2, n_chan)), dma),
        collective_id=0,
    )(own, kernel, bias.reshape(filters, 1), act_grad.reshape(filters, CELLS))
    dw, gx = call(
        functools.partial(grads_kernel, sizes, width),
        (shape(filters, 27 * width), shape(n_chan, planes, part, cells)),
        3,
        3 * flops,
        12 << 20,
        scratch=(pltpu.VMEM((filters, CELLS), BF), dma, dma),
        collective_id=2,
    )(x_all, kernel, dy)
    count = batch * sizes[0]
    rows = filters // group
    slots = pltpu.VMEM((sizes[1], rows, 27 * width), BF)
    dw_all, parts, dbs = call(
        functools.partial(share_kernel, sizes),
        (
            shape(group, rows, 27 * width),
            shape(n_chan, planes, part, cells),
            shape(group, 8, filters, dtype=F32),
        ),
        3,
        0,
        12 << 20,
        scratch=(
            slots,
            slots,
            slots,
            slots,
            dma((3, sizes[1])),
            dma((group,)),
            dma((n_chan,)),
            dma((n_chan,)),
            dma((group,)),
            dma((group,)),
            dma((3,)),
            dma((sizes[1],)),
            dma((sizes[1],)),
            dma((sizes[1],)),
            dma((sizes[1],)),
            dma((sizes[1],)),
        ),
        collective_id=1,
    )(dw.reshape(group, rows, 27 * width), gx, db)
    grad_w = dw_all.reshape(filters, 27 * width).astype(F32) / count
    grad_b = jnp.sum(dbs[:, 0], axis=0) / count
    grad_x = call(merge_kernel, shape(planes * part, cells), 2, 2 * planes * part * cells**2, 1 << 20)(
        parts, parity
    )
    return (
        act.reshape(act_grad.shape),
        grad_x.reshape(volumes.shape),
        grad_w,
        grad_b,
    )


ORDER = [(0, 1), (1, 1), (1, 2), (1, 3), (1, 0), (0, 0), (0, 2), (0, 3)]
EIGHT = ORDER.index((1, 3))
EARLY = 5
PIECES = 10
CHUNKS = [(0, 4), (4, 7), (7, 10)]
NT = (((1,), (1,)), ((), ()))
TN = (((0,), (0,)), ((), ()))


def class_of(tap):
    return ORDER.index((int(tap[0] != 1), phase_of(tap[1], tap[2])))


def share_taps(row):
    return [
        (t, tap, class_of(tap) - 4 * row)
        for k in range(4 * row, 4 * row + 4)
        for t, tap in enumerate(TAPS)
        if class_of(tap) == k and k != EIGHT
    ]


def parity_block():
    side = 2 * CELLS
    row = lax.broadcasted_iota(jnp.int32, (side, side), 0)
    col = lax.broadcasted_iota(jnp.int32, (side, side), 1)
    y, z = row // GRID, row % GRID
    dst = (2 * (y % 2) + z % 2) * (CELLS // 2) + (y // 2) * HALF + z // 2
    return jnp.where(dst == col, 1.0, 0.0).astype(BF)


class Net:
    def __init__(self, out_sem):
        self.out_sem, self.count, self.started = out_sem, 0, []

    def go(self, src, dst, in_sem, device, cond=None):
        copy = send(src, dst, self.out_sem.at[self.count], in_sem, device)
        self.count += 1
        self.started.append((copy, cond))
        if cond is None:
            copy.start()
        else:
            pl.when(cond)(copy.start)

    def wait(self, dst, in_sem, device, cond=None):
        copy = send(dst, dst, self.out_sem.at[0], in_sem, device)
        if cond is None:
            copy.wait_recv()
        else:
            pl.when(cond)(copy.wait_recv)

    def drain(self):
        for copy, cond in self.started:
            if cond is None:
                copy.wait_send()
            else:
                pl.when(cond)(copy.wait_send)


SENDS = 160


def layer_kernel(
    sizes, width, scale, v_ref, w_hbm, b_ref, g_ref,
    act_ref, gx_ref, dwb_ref, d8_ref, db_ref,
    w2, xg, xb, x8, acc, carry, dysh, dyt, gx_far, gx_in, gx_own,
    out_sem, local_sem, g_in, b_in, e_in, e_all, dy_in, dyt_in, dw_in, gx_sem, misc_in,
):
    n_dp, n_space, n_chan = sizes
    blocks = n_dp * n_space
    y, z, c = place()
    chip, core = c // 2, c % 2
    b = y * n_space + z
    twin = (y, z, 2 * chip + 1 - core)
    far = (y, z, 2 * (1 - chip) + core)
    cf = 2 * (1 - chip) + core
    right = (y, jnp.minimum(z + 1, n_space - 1), c)
    left = (y, jnp.maximum(z - 1, 0), c)
    across = (1 - y, z, c)
    net = Net(out_sem)

    barrier = pltpu.get_barrier_semaphore()
    for device in (twin, far):
        pl.semaphore_signal(barrier, 1, device_id=device, device_id_type=pl.DeviceIdType.MESH)
    for o in range(1, blocks):
        h = (b + o) % blocks
        pl.semaphore_signal(
            barrier, 1, device_id=(h // n_space, h % n_space, c), device_id_type=pl.DeviceIdType.MESH
        )
    own_w = pltpu.make_async_copy(w_hbm, w2.at[0], local_sem.at[0])
    own_w.start()

    part = v_ref.shape[1]
    half = CELLS // 2
    parity = parity_block()
    for h in range(2):
        r = jnp.dot(
            v_ref[:, :, 2 * CELLS * h : 2 * CELLS * (h + 1)].reshape(2 * part, 2 * CELLS), parity,
            preferred_element_type=F32,
        ).astype(BF)
        for k, (p, ph) in enumerate(ORDER):
            tile = r[p * part : (p + 1) * part, ph * half : (ph + 1) * half]
            xg[c, k, :, h * half : (h + 1) * half] = tile
            if k == EIGHT:
                x8[c, b, :, h * half : (h + 1) * half] = tile

    pl.semaphore_wait(barrier, blocks + 1)

    spans = [pl.ds(0, EARLY), pl.ds(EARLY, 8 - EARLY)]
    for m in range(2):
        block = xg.at[c, spans[m]]
        net.go(block, block, g_in.at[m, c], far)
        net.go(block, block, g_in.at[m, c], twin)

    def chain_start(ref, sem):
        net.go(ref, ref, sem, right, z < n_space - 1)
        net.go(ref, ref, sem, left, z > 0)
        net.go(ref, ref, sem, across)

    def chain_step(d, ref_of, sem_of, then=None):
        for ok, zz, on, onward in (
            (z - d >= 0, jnp.maximum(z - d, 0), right, z < n_space - 1),
            (z + d < n_space, jnp.minimum(z + d, n_space - 1), left, z > 0),
        ):
            s = y * n_space + zz
            net.wait(ref_of(s), sem_of(s), left, ok)
            net.go(ref_of(s), ref_of(s), sem_of(s), on, ok & onward)
            net.go(ref_of(s), ref_of(s), sem_of(s), across, ok)
            if then is not None:
                pl.when(ok)(functools.partial(then, s))

    def chain_end(zz, ref_of, sem_of, then=None):
        s = (1 - y) * n_space + zz
        net.wait(ref_of(s), sem_of(s), across)
        if then is not None:
            then(s)

    rows = part // 2
    for row in range(n_dp):
        for zl in range(2):
            to = (row, 2 * core + zl, c)
            net.go(
                xg.at[c, pl.ds(4 * row, 4), pl.ds(rows * zl, rows)], xb.at[chip, b], b_in.at[chip, b], to,
                jnp.logical_not((y == row) & (z == 2 * core + zl)),
            )

    def eight(s):
        return x8.at[c, s]

    def eight_sem(s):
        return e_in.at[s]

    chain_start(x8.at[c, b], e_in.at[b])
    net.go(w_hbm, w2.at[1], misc_in.at[0], twin)
    own_w.wait()

    def columns(t, first, count):
        return pl.ds(pl.multiple_of(t * width + first * part, 128), count * part)

    def forward_part(ch, ready, group, s, first):
        total = None if first else acc[4 * group + s]
        for t, tap in enumerate(TAPS):
            k = class_of(tap)
            if shift_of(tap[1], tap[2]) != s or (tap[0] == 0) != (group == 0) or k not in ready:
                continue
            term = jnp.dot(
                w2[0, :, columns(t, 2 * ch, 2)],
                xg[pl.ds(2 * ch, 2), k].reshape(2 * part, CELLS),
                preferred_element_type=F32,
            )
            total = term if total is None else total + term
        acc[4 * group + s] = total

    for m in range(2):
        net.wait(xg.at[twin[2], spans[m]], g_in.at[m, twin[2]], twin)
    for s in range(4):
        for group in range(2):
            forward_part(chip, range(8), group, s, True)
    chain_step(1, eight, eight_sem)
    early, late = range(EARLY), range(EARLY, 8)
    other = 2 * (1 - chip) + 1 - core

    def far_arrived(m):
        net.wait(xg.at[cf, spans[m]], g_in.at[m, cf], far)
        net.go(xg.at[cf, spans[m]], xg.at[cf, spans[m]], g_in.at[m, cf], twin)
        net.wait(xg.at[other, spans[m]], g_in.at[m, other], twin)

    far_arrived(0)
    for s in range(4):
        forward_part(1 - chip, early, 0, s, False)
    ahead = acc[0]
    for s in (1, 2, 3):
        ahead = ahead + forward_shift(acc[s], s)
    carry[0] = ahead
    net.go(carry.at[0], carry.at[1], misc_in.at[1], right, z < n_space - 1)
    for s in range(4):
        forward_part(1 - chip, early, 1, s, False)
    chain_step(2, eight, eight_sem)
    far_arrived(1)

    relay = core == z // 2

    def relay_share(o):
        s = (b + o) % blocks
        net.wait(xb.at[chip, s], b_in.at[chip, s], across, relay)
        net.go(xb.at[chip, s], xb.at[chip, s], b_in.at[chip, s], far, relay)
        net.go(xb.at[chip, s], xb.at[chip, s], b_in.at[chip, s], twin, relay)

    for s in range(4):
        forward_part(1 - chip, late, 1, s, False)
    u = b_ref[...] + acc[4]
    for s in (1, 2, 3):
        u = u + forward_shift(acc[4 + s], s)

    @pl.when(z == 0)
    def _():
        carry[1] = jnp.zeros_like(carry[1])

    net.wait(carry.at[1], misc_in.at[1], left, z > 0)
    u = u + carry[1]
    k0 = 0.7978845608028654
    th = jnp.tanh(k0 * (u + 0.044715 * (u * u * u)))
    slope = 0.5 * (1.0 + th) + 0.5 * u * (1.0 - th * th) * k0 * (1.0 + 3 * 0.044715 * u * u)
    dysh[0, b] = (g_ref[...].astype(F32) * slope).astype(BF)
    act_ref[...] = (0.5 * u * (1.0 + th)).astype(BF)

    def dy_of(s):
        return dysh.at[0, s]

    def dy_sem(s):
        return dy_in.at[s]

    chain_start(dysh.at[0, b], dy_in.at[b])
    net.go(dysh.at[0, b], dyt.at[0, 0], dyt_in.at[0], twin)
    for o in range(1, blocks):
        relay_share(o)
    own_slots = []
    for hx in range(2):
        own_slots.append(
            pltpu.make_async_copy(
                xg.at[2 * hx + z // 2, pl.ds(4 * y, 4), pl.ds(pl.multiple_of(rows * (z % 2), rows), rows)],
                xb.at[hx, b],
                local_sem.at[1 + hx],
            )
        )
        own_slots[-1].start()

    def shift_slot(s):
        wide = dysh[0, s].astype(F32)
        for k in (1, 2, 3):
            dysh[k, s] = backward_shift(wide, k).astype(BF)

    shift_slot(b)
    chain_step(1, dy_of, dy_sem, shift_slot)
    nxt = y * n_space + jnp.minimum(z + 1, n_space - 1)
    net.go(dysh.at[0, nxt], dyt.at[0, 1], dyt_in.at[1], twin, z < n_space - 1)
    chain_step(3, eight, eight_sem)
    chain_step(2, dy_of, dy_sem, shift_slot)
    for zz in range(n_space):
        chain_end(zz, eight, eight_sem)
    chain_step(3, dy_of, dy_sem, shift_slot)
    for zz in range(n_space):
        chain_end(zz, dy_of, dy_sem, shift_slot)

    for r in range(n_dp):
        mine = x8.at[c, pl.ds(n_space * r, n_space)]
        net.go(mine, mine, e_all.at[r, c], far)
        net.go(mine, mine, e_all.at[r, c], twin)

    for o in range(1, blocks):
        s = (b + o) % blocks
        other_half = xb.at[1 - chip, s]
        net.wait(other_half, b_in.at[1 - chip, s], far, relay)
        net.go(other_half, other_half, b_in.at[1 - chip, s], twin, relay)
    for o in range(1, blocks):
        s = (b + o) % blocks
        for hx in range(2):
            net.wait(xb.at[hx, s], b_in.at[hx, s], twin, jnp.logical_not(relay))
    for copy in own_slots:
        copy.wait()

    def share_piece(row, i):
        taps = share_taps(row)
        if i >= len(taps):
            dwb_ref[b, i] = jnp.zeros(dwb_ref.shape[2:], BF)
            return
        _, (k1, k2, k3), k = taps[i]
        total = None
        for v in range(n_dp):
            for zz in range(n_space - (k1 == 0)):
                s = v * n_space + zz
                term = lax.dot_general(
                    dysh[shift_of(k2, k3), s + (k1 == 0)],
                    xb[:, s, k].reshape(part, CELLS),
                    NT,
                    preferred_element_type=F32,
                )
                total = term if total is None else total + term
        dwb_ref[b, i] = (total * scale).astype(BF)

    def dw_of(m):
        lo, hi = CHUNKS[m]
        return lambda s: dwb_ref.at[s, pl.ds(lo, hi - lo)]

    def dw_sem(m):
        return lambda s: dw_in.at[m, s]

    for m, (lo, hi) in enumerate(CHUNKS):
        for row in range(n_dp):
            @pl.when(y == row)
            def _():
                for i in range(lo, hi):
                    share_piece(row, i)
        chain_start(dw_of(m)(b), dw_sem(m)(b))

    @pl.when(z == n_space - 1)
    def _():
        dyt[0, 1] = jnp.zeros_like(dyt[0, 1])

    net.wait(dyt.at[0, 0], dyt_in.at[0], twin)
    net.wait(dyt.at[0, 1], dyt_in.at[1], twin, z < n_space - 1)
    for i in range(2):
        wide = dyt[0, i].astype(F32)
        for k in (1, 2, 3):
            dyt[k, i] = backward_shift(wide, k).astype(BF)
    net.wait(w2.at[1], misc_in.at[0], twin)
    edge = jnp.where(z < n_space - 1, 1.0, 0.0).astype(BF)

    def input_grad(j, p, ph):
        total = None
        for t, (k1, k2, k3) in enumerate(TAPS):
            if phase_of(k2, k3) != ph or (k1 != 1) != (p == 1):
                continue
            s = shift_of(k2, k3)
            here = dysh[s, nxt] * edge if k1 == 0 else dysh[s, b]
            for i, view in enumerate((here, dyt[s, int(k1 == 0)])):
                term = lax.dot_general(
                    w2[i, :, columns(t, j, 1)], view, TN, preferred_element_type=F32
                )
                total = term if total is None else total + term
        return total

    for p in range(2):
        for ph in range(4):
            gx_far[p, ph] = input_grad(cf, p, ph).astype(BF)
        net.go(gx_far.at[p], gx_in.at[p], gx_sem.at[p], far)
        for m in range(len(CHUNKS)):
            if p == 0:
                chain_step(1, dw_of(m), dw_sem(m))
    for p in range(2):
        for ph in range(4):
            gx_own[p, ph] = input_grad(c, p, ph)
    for m in range(len(CHUNKS)):
        chain_step(2, dw_of(m), dw_sem(m))

    for r in range(n_dp):
        theirs = x8.at[cf, pl.ds(n_space * r, n_space)]
        net.wait(theirs, e_all.at[r, cf], far)
        net.go(theirs, theirs, e_all.at[r, cf], twin)
    for r in range(n_dp):
        for j in (twin[2], other):
            net.wait(x8.at[j, pl.ds(n_space * r, n_space)], e_all.at[r, j], twin)
    for k in range(2):
        for v in range(n_dp):
            for zz in range(n_space - (k == 0)):
                s = v * n_space + zz
                term = lax.dot_general(
                    dysh[:, s + (k == 0)].reshape(4 * part, CELLS),
                    x8[:, s].reshape(n_chan * part, CELLS),
                    NT,
                    preferred_element_type=F32,
                ) * scale
                if s == 0:
                    d8_ref[k] = term
                else:
                    d8_ref[k] += term
    for m in range(len(CHUNKS)):
        chain_step(3, dw_of(m), dw_sem(m))
    ones = jnp.ones((8, CELLS), BF)
    total = None
    for s in range(blocks):
        term = lax.dot_general(ones, dysh[0, s], NT, preferred_element_type=F32)
        total = term if total is None else total + term
    db_ref[...] = total * scale

    for p in range(2):
        net.wait(gx_in.at[p], gx_sem.at[p], far)
    for p in range(2):
        cells = [(gx_own[p, ph] + gx_in[p, ph].astype(F32)).astype(BF) for ph in range(4)]
        for h in range(2):
            strip = jnp.concatenate([cell[:, h * half : (h + 1) * half] for cell in cells], axis=1)
            gx_ref[p, :, 2 * CELLS * h : 2 * CELLS * (h + 1)] = lax.dot_general(
                strip, parity_block(), NT, preferred_element_type=F32
            ).astype(BF)
    for m in range(len(CHUNKS)):
        for zz in range(n_space):
            chain_end(zz, dw_of(m), dw_sem(m))
    net.drain()


def finish_kernel(n_space, part, dwb_ref, d8_ref, gx_ref, act_ref, db_ref, act_out, gx_out, dw_out, db_out, wide, sem):
    act_out[...] = act_ref[...]
    gx_out[...] = gx_ref[...]
    db_out[...] = db_ref[...]
    width = 4 * part
    where = {}
    for row in range(2):
        for i, (t, _, _) in enumerate(share_taps(row)):
            where[t] = (row, i)
    copies = []
    low = lax.broadcasted_iota(jnp.int32, (part, part), 1) < part // 2
    for t, (k1, k2, k3) in enumerate(TAPS):
        first = t * width
        if t in where:
            row, i = where[t]
            for q in range(2):
                even = dwb_ref[row * n_space + 2 * q, i].astype(F32)
                odd = dwb_ref[row * n_space + 2 * q + 1, i].astype(F32)
                wide[:, first + q * part : first + (q + 1) * part] = jnp.where(low, even, pltpu.roll(odd, part // 2, 1))
                wide[:, first + (2 + q) * part : first + (3 + q) * part] = jnp.where(
                    low, pltpu.roll(even, part // 2, 1), odd
                )
        else:
            s = shift_of(k2, k3)
            wide[:, first : first + width] = d8_ref[int(k1 == 2), s * part : (s + 1) * part]
        span = pl.ds(first, width)
        copies.append(pltpu.make_async_copy(wide.at[:, span], dw_out.at[:, span], sem.at[t]))
        copies[-1].start()
    for copy in copies:
        copy.wait()


def per_device_shared(volumes, kernel, bias, act_grad):
    batch, planes, part, cells = volumes.shape
    filters = kernel.shape[0]
    width = kernel.shape[1] // 27
    sizes = tuple(lax.axis_size(a) for a in ("dp", "space", "chan"))
    n_dp, n_space, n_chan = sizes
    blocks = n_dp * n_space
    dma = pltpu.SemaphoreType.DMA
    flops = 2 * 27 * width * filters * CELLS
    ANY = pl.BlockSpec(memory_space=pl.ANY)
    act, gx, dwb, d8, db = pl.pallas_call(
        functools.partial(layer_kernel, sizes, width, 1.0 / (batch * n_dp)),
        out_shape=(
            shape(filters, CELLS),
            shape(planes, part, cells),
            shape(blocks, PIECES, filters, part),
            shape(2, 4 * filters, width, dtype=F32),
            shape(8, filters, dtype=F32),
        ),
        in_specs=[VM, ANY, VM, VM],
        out_specs=[VM] * 5,
        scratch_shapes=(
            pltpu.VMEM((2, filters, 27 * width), BF),
            pltpu.VMEM((n_chan, 8, part, CELLS), BF),
            pltpu.VMEM((2, blocks, 4, part // 2, CELLS), BF),
            pltpu.VMEM((n_chan, blocks, part, CELLS), BF),
            pltpu.VMEM((8, filters, CELLS), F32),
            pltpu.VMEM((2, filters, CELLS), F32),
            pltpu.VMEM((4, blocks, filters, CELLS), BF),
            pltpu.VMEM((4, 2, filters, CELLS), BF),
            pltpu.VMEM((2, 4, part, CELLS), BF),
            pltpu.VMEM((2, 4, part, CELLS), BF),
            pltpu.VMEM((2, 4, part, CELLS), F32),
            dma((SENDS,)),
            dma((3,)),
            dma((2, n_chan)),
            dma((2, blocks)),
            dma((blocks,)),
            dma((n_dp, n_chan)),
            dma((blocks,)),
            dma((2,)),
            dma((len(CHUNKS), blocks)),
            dma((2,)),
            dma((2,)),
        ),
        compiler_params=pltpu.CompilerParams(
            vmem_limit_bytes=56 << 20, collective_id=0, has_side_effects=True
        ),
        cost_estimate=pl.CostEstimate(flops=5 * flops, bytes_accessed=12 << 20, transcendentals=0),
    )(volumes.reshape(planes, part, cells), kernel, bias.reshape(filters, 1), act_grad.reshape(filters, CELLS))
    act, gx, dw, db = pl.pallas_call(
        functools.partial(finish_kernel, n_space, part),
        out_shape=(
            shape(filters, CELLS),
            shape(planes, part, cells),
            shape(filters, 27 * width, dtype=F32),
            shape(8, filters, dtype=F32),
        ),
        in_specs=[VM] * 5,
        out_specs=[VM, VM, ANY, VM],
        scratch_shapes=(pltpu.VMEM((filters, 27 * width), F32), dma((27,))),
        compiler_params=pltpu.CompilerParams(vmem_limit_bytes=40 << 20),
        cost_estimate=pl.CostEstimate(flops=0, bytes_accessed=12 << 20, transcendentals=0),
    )(dwb, d8, gx, act, db)
    return act.reshape(act_grad.shape), gx.reshape(volumes.shape), dw, db[0]


def solution(mesh):
    shared = (mesh.shape["dp"], mesh.shape["space"], mesh.shape["chan"]) == (2, 4, 4)
    in_specs = (
        P("dp", "space", "chan", None),
        P("chan", None),
        P("chan"),
        P("dp", "space", "chan", None),
    )
    out_specs = (
        P("dp", "space", "chan", None),
        P("dp", "space", "chan", None),
        P("chan", None),
        P("chan"),
    )
    return jax.shard_map(
        per_device_shared if shared else per_device,
        mesh=mesh, in_specs=in_specs, out_specs=out_specs, check_vma=False,
    )
```

```python
import functools

import jax
import jax.numpy as jnp
from jax import lax
from jax.experimental import pallas as pl
from jax.experimental.pallas import tpu as pltpu
from jax.sharding import PartitionSpec as P

GRID = 32
HALF = GRID // 2
CELLS = HALF * HALF
BF = jnp.bfloat16
F32 = jnp.float32
VM = pl.BlockSpec(memory_space=pltpu.VMEM)
TAPS = [(k1, k2, k3) for k1 in range(3) for k2 in range(3) for k3 in range(3)]


def phase_of(k2, k3):
    return 2 * (k2 != 1) + (k3 != 1)


def shift_of(k2, k3):
    return 2 * (k2 == 0) + (k3 == 0)


def parity_matrix():
    full = GRID * GRID
    dst = lax.broadcasted_iota(jnp.int32, (1, full), 1)
    phase, cell = dst // CELLS, dst % CELLS
    y = 2 * (cell // HALF) + phase // 2
    z = 2 * (cell % HALF) + phase % 2
    src = y * GRID + z
    rows = lax.broadcasted_iota(jnp.int32, (full, full), 0)
    return jnp.where(rows == src, 1.0, 0.0).astype(BF)


def lanes():
    return lax.broadcasted_iota(jnp.int32, (1, CELLS), 1)


def forward_shift(x, s):
    if s & 2:
        x = jnp.where(lanes() >= HALF, pltpu.roll(x, HALF, 1), 0.0)
    if s & 1:
        x = jnp.where(lanes() % HALF != 0, pltpu.roll(x, 1, 1), 0.0)
    return x


def backward_shift(x, s):
    if s & 2:
        x = jnp.where(lanes() < CELLS - HALF, pltpu.roll(x, CELLS - HALF, 1), 0.0)
    if s & 1:
        x = jnp.where(lanes() % HALF != HALF - 1, pltpu.roll(x, CELLS - 1, 1), 0.0)
    return x


def split_kernel(v_ref, p_ref, o_ref):
    o_ref[...] = jnp.dot(v_ref[...], p_ref[...], preferred_element_type=F32).astype(BF)


def merge_kernel(v_ref, p_ref, o_ref):
    total = v_ref[0].astype(F32)
    for j in range(1, v_ref.shape[0]):
        total = total + v_ref[j].astype(F32)
    o_ref[...] = lax.dot_general(
        total.astype(BF).reshape(o_ref.shape), p_ref[...], (((1,), (1,)), ((), ())), preferred_element_type=F32
    ).astype(BF)


def send(src, dst, send_sem, recv_sem, device):
    return pltpu.make_async_remote_copy(
        src, dst, send_sem, recv_sem, device_id=device, device_id_type=pl.DeviceIdType.MESH
    )


def place():
    return lax.axis_index("dp"), lax.axis_index("space"), lax.axis_index("chan")


def greet(sizes):
    n_dp, n_space, n_chan = sizes
    y, z, c = place()
    barrier = pltpu.get_barrier_semaphore()
    g = y * n_space + z
    for o in range(1, n_chan):
        pl.semaphore_signal(
            barrier, 1, device_id=(y, z, (c + o) % n_chan), device_id_type=pl.DeviceIdType.MESH
        )
    for o in range(1, n_dp * n_space):
        h = (g + o) % (n_dp * n_space)
        pl.semaphore_signal(
            barrier, 1, device_id=(h // n_space, h % n_space, c), device_id_type=pl.DeviceIdType.MESH
        )
    pl.semaphore_wait(barrier, n_chan + n_dp * n_space - 2)


def gather_inputs(sizes, own_ref, x_ref, out_sem, in_sem, local_sem):
    n_dp, n_space, n_chan = sizes
    chips = n_chan // 2
    y, z, c = place()
    chip, core = c // 2, c % 2
    twin = (y, z, 2 * chip + 1 - core)
    greet(sizes)

    def planes(k):
        return pl.ds(1, 2) if k else pl.ds(0, 1)

    def block(k, j):
        return x_ref.at[planes(k), j]

    def to_chip(k, o, src):
        return send(
            src, block(k, c), out_sem.at[k, 0, o], in_sem.at[k, c],
            (y, z, 2 * ((chip + o) % chips) + core),
        )

    def to_twin(k, o, src):
        j = 2 * ((chip - o + chips) % chips) + core
        return send(src, block(k, j), out_sem.at[k, 1, o], in_sem.at[k, j], twin)

    def arrived(k, j):
        send(block(k, j), block(k, j), out_sem.at[k, 1, 0], in_sem.at[k, j], twin).wait_recv()

    rim = send(own_ref.at[pl.ds(1, 1)], block(0, c), out_sem.at[0, 2, 0], in_sem.at[0, c], (y, jnp.minimum(z + 1, n_space - 1), c))
    sends = [to_chip(1, o, own_ref) for o in range(1, chips)] + [to_twin(1, 0, own_ref)]

    @pl.when(z < n_space - 1)
    def _():
        rim.start()

    for copy in sends:
        copy.start()
    keep = pltpu.make_async_copy(own_ref, block(1, c), local_sem)
    keep.start()

    rim_out = [to_chip(0, o, block(0, c)) for o in range(1, chips)] + [to_twin(0, 0, block(0, c))]

    @pl.when(z > 0)
    def _():
        arrived(0, c)
        for copy in rim_out:
            copy.start()

    @pl.when(z == 0)
    def _():
        x_ref[0] = jnp.zeros_like(x_ref[0])

    for o in range(1, chips):
        j = 2 * ((chip - o + chips) % chips) + core
        arrived(1, j)
        passed = to_twin(1, o, block(1, j))
        passed.start()
        sends.append(passed)

    @pl.when(z > 0)
    def _():
        for o in range(1, chips):
            j = 2 * ((chip - o + chips) % chips) + core
            arrived(0, j)
            passed = to_twin(0, o, block(0, j))
            passed.start()
            rim_out.append(passed)
        for o in range(chips):
            arrived(0, 2 * ((chip - o + chips) % chips) + 1 - core)
        for copy in rim_out:
            copy.wait_send()

    for o in range(chips):
        arrived(1, 2 * ((chip - o + chips) % chips) + 1 - core)
    for copy in sends:
        copy.wait_send()

    @pl.when(z < n_space - 1)
    def _():
        rim.wait_send()

    keep.wait()


def forward_kernel(
    sizes, width, own_ref, w_ref, b_ref, g_ref, x_ref, act_ref, dy_ref, db_ref, out_sem, in_sem, local_sem
):
    gather_inputs(sizes, own_ref, x_ref, out_sem, in_sem, local_sem)
    sums = [None] * 4
    for t, (k1, k2, k3) in enumerate(TAPS):
        ph, s = phase_of(k2, k3), shift_of(k2, k3)
        part = jnp.dot(
            w_ref[:, t * width : (t + 1) * width],
            x_ref[k1, :, :, ph * CELLS : (ph + 1) * CELLS].reshape(width, CELLS),
            preferred_element_type=F32,
        )
        sums[s] = part if sums[s] is None else sums[s] + part
    u = b_ref[...] + sums[0]
    for s in (1, 2, 3):
        u = u + forward_shift(sums[s], s)
    c = 0.7978845608028654
    th = jnp.tanh(c * (u + 0.044715 * (u * u * u)))
    act_ref[...] = (0.5 * u * (1.0 + th)).astype(BF)
    slope = 0.5 * (1.0 + th) + 0.5 * u * (1.0 - th * th) * c * (1.0 + 3 * 0.044715 * u * u)
    dy = (g_ref[...].astype(F32) * slope).astype(BF)
    dy_ref[...] = dy
    db_ref[...] = lax.dot_general(
        jnp.ones((8, CELLS), BF), dy, (((1,), (1,)), ((), ())), preferred_element_type=F32
    )


def shifted(dy):
    wide = dy.astype(F32)
    return [dy] + [backward_shift(wide, s).astype(BF) for s in (1, 2, 3)]


def grads_kernel(sizes, width, x_ref, w_ref, dy_ref, dw_ref, gx_ref, next_ref, out_sem, in_sem):
    n_space = sizes[1]
    y, z, c = place()
    greet(sizes)
    back = send(dy_ref, next_ref, out_sem, in_sem, (y, jnp.maximum(z - 1, 0), c))

    @pl.when(z > 0)
    def _():
        back.start()

    own = shifted(dy_ref[...])
    for t, (k1, k2, k3) in enumerate(TAPS):
        ph, s = phase_of(k2, k3), shift_of(k2, k3)
        part = lax.dot_general(
            own[s],
            x_ref[k1, :, :, ph * CELLS : (ph + 1) * CELLS].reshape(width, CELLS),
            (((1,), (1,)), ((), ())),
            preferred_element_type=F32,
        )
        dw_ref[:, t * width : (t + 1) * width] = part.astype(BF)

    @pl.when(z < n_space - 1)
    def _():
        back.wait_recv()

    @pl.when(z == n_space - 1)
    def _():
        next_ref[...] = jnp.zeros_like(next_ref)

    following = shifted(next_ref[...])
    for plane in range(2):
        for ph in range(4):
            total = None
            for t, (k1, k2, k3) in enumerate(TAPS):
                if phase_of(k2, k3) != ph or (k1 == 1) != (plane == 0):
                    continue
                views = following if k1 == 0 else own
                part = lax.dot_general(
                    w_ref[:, t * width : (t + 1) * width],
                    views[shift_of(k2, k3)],
                    (((0,), (0,)), ((), ())),
                    preferred_element_type=F32,
                )
                total = part if total is None else total + part
            gx_ref[:, plane, :, ph * CELLS : (ph + 1) * CELLS] = total.astype(BF).reshape(
                gx_ref.shape[0], gx_ref.shape[2], CELLS
            )

    @pl.when(z > 0)
    def _():
        back.wait_send()


def share_kernel(
    sizes, dw_ref, gx_ref, db_ref, all_ref, parts_ref, dbs_ref, y_ref, r_ref, l_ref, s_ref,
    out_sem, in_sem, gx_out, gx_in, db_out, db_in, local_sem, y_out, y_in, z_out, r_in, l_in
):
    n_dp, n_space, n_chan = sizes
    group = n_dp * n_space
    y, z, c = place()
    g = y * n_space + z
    greet(sizes)
    right = (y, jnp.minimum(z + 1, n_space - 1), c)
    left = (y, jnp.maximum(z - 1, 0), c)
    across = (1 - y, z, c)

    def hop(way, device, j, src=None):
        slot = all_ref.at[y * n_space + j]
        return send(slot if src is None else src, slot, out_sem.at[way, j], in_sem.at[y * n_space + j], device)

    def arrived(h):
        send(all_ref.at[h], all_ref.at[h], out_sem.at[2, 0], in_sem.at[h], across).wait_recv()

    locals_ = [
        pltpu.make_async_copy(gx_ref.at[c], parts_ref.at[c], local_sem.at[1]),
        pltpu.make_async_copy(db_ref, dbs_ref.at[g], local_sem.at[2]),
    ]

    def over(j):
        return send(dw_ref.at[(1 - y) * n_space + j], y_ref.at[j], y_out.at[j], y_in.at[j], across)

    def rightward(j):
        return send(s_ref.at[j], r_ref.at[j], z_out.at[j], r_in.at[j], right)

    def leftward(j):
        return send(s_ref.at[j], l_ref.at[j], z_out.at[j], l_in.at[j], left)

    def both(j):
        over(j).wait_recv()
        return dw_ref[y * n_space + j].astype(F32) + y_ref[j].astype(F32)

    for d in range(n_space - 1, 0, -1):
        @pl.when(z + d < n_space)
        def _():
            over(jnp.minimum(z + d, n_space - 1)).start()

        @pl.when(z - d >= 0)
        def _():
            over(jnp.maximum(z - d, 0)).start()

    over(z).start()
    extra = []
    for o in range(1, n_chan):
        to = (c + o) % n_chan
        extra.append(
            send(gx_ref.at[to], parts_ref.at[c], gx_out.at[o], gx_in.at[o], (y, z, to))
        )
    for o in range(1, group):
        to = (g + o) % group
        extra.append(
            send(db_ref, dbs_ref.at[g], db_out.at[o], db_in.at[o], (to // n_space, to % n_space, c))
        )
    for copy in extra:
        copy.start()
    for copy in locals_:
        copy.start()

    for d in range(n_space - 1, 0, -1):
        @pl.when(z + d < n_space)
        def _():
            j = jnp.minimum(z + d, n_space - 1)
            mine = both(j)

            @pl.when(z == 0)
            def _():
                s_ref[j] = mine.astype(BF)

            @pl.when(z > 0)
            def _():
                rightward(j).wait_recv()
                s_ref[j] = (mine + r_ref[j].astype(F32)).astype(BF)

            rightward(j).start()

        @pl.when(z - d >= 0)
        def _():
            j = jnp.maximum(z - d, 0)
            mine = both(j)

            @pl.when(z == n_space - 1)
            def _():
                s_ref[j] = mine.astype(BF)

            @pl.when(z < n_space - 1)
            def _():
                leftward(j).wait_recv()
                s_ref[j] = (mine + l_ref[j].astype(F32)).astype(BF)

            leftward(j).start()

    @pl.when(z == 0)
    def _():
        r_ref[z] = jnp.zeros_like(r_ref[z])

    @pl.when(z == n_space - 1)
    def _():
        l_ref[z] = jnp.zeros_like(l_ref[z])

    @pl.when(z > 0)
    def _():
        rightward(z).wait_recv()

    @pl.when(z < n_space - 1)
    def _():
        leftward(z).wait_recv()

    all_ref[g] = (both(z) + r_ref[z].astype(F32) + l_ref[z].astype(F32)).astype(BF)

    @pl.when(z < n_space - 1)
    def _():
        hop(0, right, z).start()

    @pl.when(z > 0)
    def _():
        hop(1, left, z).start()

    hop(2, across, z).start()

    for d in range(1, n_space):
        @pl.when(z - d >= 0)
        def _():
            j = jnp.maximum(z - d, 0)
            arrived(y * n_space + j)

            @pl.when(z < n_space - 1)
            def _():
                hop(0, right, j).start()

            hop(2, across, j).start()

        @pl.when(z + d < n_space)
        def _():
            j = jnp.minimum(z + d, n_space - 1)
            arrived(y * n_space + j)

            @pl.when(z > 0)
            def _():
                hop(1, left, j).start()

            hop(2, across, j).start()

    for o in range(1, n_chan):
        frm = (c - o + n_chan) % n_chan
        send(parts_ref.at[frm], parts_ref.at[frm], gx_out.at[o], gx_in.at[o], (y, z, frm)).wait_recv()
    for o in range(1, group):
        frm = (g - o + group) % group
        send(dbs_ref.at[frm], dbs_ref.at[frm], db_out.at[o], db_in.at[o], (frm // n_space, frm % n_space, c)).wait_recv()
    for j in range(n_space):
        arrived((1 - y) * n_space + j)
        hop(2, across, j).wait_send()

        @pl.when((j <= z) & (z < n_space - 1))
        def _():
            hop(0, right, j).wait_send()

        @pl.when((j >= z) & (z > 0))
        def _():
            hop(1, left, j).wait_send()

        over(j).wait_send()

        @pl.when(j > z)
        def _():
            rightward(j).wait_send()

        @pl.when(j < z)
        def _():
            leftward(j).wait_send()

    for copy in extra:
        copy.wait_send()
    for copy in locals_:
        copy.wait()


def call(kernel, out_shape, n_in, flops, moved, scratch=(), collective_id=None):
    many = isinstance(out_shape, (tuple, list))
    return pl.pallas_call(
        kernel,
        out_shape=out_shape,
        in_specs=[VM] * n_in,
        out_specs=[VM] * len(out_shape) if many else VM,
        scratch_shapes=scratch,
        compiler_params=pltpu.CompilerParams(
            vmem_limit_bytes=48 << 20,
            collective_id=collective_id,
            has_side_effects=collective_id is not None,
        ),
        cost_estimate=pl.CostEstimate(flops=flops, bytes_accessed=moved, transcendentals=0),
    )


def shape(*dims, dtype=BF):
    return jax.ShapeDtypeStruct(dims, dtype)


def per_device(volumes, kernel, bias, act_grad):
    batch, planes, part, cells = volumes.shape
    filters = kernel.shape[0]
    width = kernel.shape[1] // 27
    parity = parity_matrix()
    own = call(split_kernel, shape(planes * part, cells), 2, 2 * planes * part * cells**2, 1 << 20)(
        volumes.reshape(planes * part, cells), parity
    ).reshape(planes, part, cells)
    sizes = tuple(lax.axis_size(a) for a in ("dp", "space", "chan"))
    group, n_chan = sizes[0] * sizes[1], sizes[2]
    dma = pltpu.SemaphoreType.DMA
    flops = 2 * 27 * width * filters * CELLS
    x_all, act, dy, db = call(
        functools.partial(forward_kernel, sizes, width),
        (
            shape(3, n_chan, part, cells),
            shape(filters, CELLS),
            shape(filters, CELLS),
            shape(8, filters, dtype=F32),
        ),
        4,
        flops,
        10 << 20,
        scratch=(dma((2, 3, n_chan // 2)), dma((2, n_chan)), dma),
        collective_id=0,
    )(own, kernel, bias.reshape(filters, 1), act_grad.reshape(filters, CELLS))
    dw, gx = call(
        functools.partial(grads_kernel, sizes, width),
        (shape(filters, 27 * width), shape(n_chan, planes, part, cells)),
        3,
        3 * flops,
        12 << 20,
        scratch=(pltpu.VMEM((filters, CELLS), BF), dma, dma),
        collective_id=2,
    )(x_all, kernel, dy)
    count = batch * sizes[0]
    rows = filters // group
    slots = pltpu.VMEM((sizes[1], rows, 27 * width), BF)
    dw_all, parts, dbs = call(
        functools.partial(share_kernel, sizes),
        (
            shape(group, rows, 27 * width),
            shape(n_chan, planes, part, cells),
            shape(group, 8, filters, dtype=F32),
        ),
        3,
        0,
        12 << 20,
        scratch=(
            slots,
            slots,
            slots,
            slots,
            dma((3, sizes[1])),
            dma((group,)),
            dma((n_chan,)),
            dma((n_chan,)),
            dma((group,)),
            dma((group,)),
            dma((3,)),
            dma((sizes[1],)),
            dma((sizes[1],)),
            dma((sizes[1],)),
            dma((sizes[1],)),
            dma((sizes[1],)),
        ),
        collective_id=1,
    )(dw.reshape(group, rows, 27 * width), gx, db)
    grad_w = dw_all.reshape(filters, 27 * width).astype(F32) / count
    grad_b = jnp.sum(dbs[:, 0], axis=0) / count
    grad_x = call(merge_kernel, shape(planes * part, cells), 2, 2 * planes * part * cells**2, 1 << 20)(
        parts, parity
    )
    return (
        act.reshape(act_grad.shape),
        grad_x.reshape(volumes.shape),
        grad_w,
        grad_b,
    )


ORDER = [(0, 1), (1, 1), (1, 2), (1, 3), (1, 0), (0, 0), (0, 2), (0, 3)]
EIGHT = ORDER.index((1, 3))
EARLY = 5
PIECES = 10
CHUNKS = [(0, 2), (2, 5), (5, 7), (7, 10)]
NT = (((1,), (1,)), ((), ()))
TN = (((0,), (0,)), ((), ()))


def class_of(tap):
    return ORDER.index((int(tap[0] != 1), phase_of(tap[1], tap[2])))


def share_taps(row):
    return [
        (t, tap, class_of(tap) - 4 * row)
        for k in range(4 * row, 4 * row + 4)
        for t, tap in enumerate(TAPS)
        if class_of(tap) == k and k != EIGHT
    ]


def parity_block():
    side = 2 * CELLS
    row = lax.broadcasted_iota(jnp.int32, (side, side), 0)
    col = lax.broadcasted_iota(jnp.int32, (side, side), 1)
    y, z = row // GRID, row % GRID
    dst = (2 * (y % 2) + z % 2) * (CELLS // 2) + (y // 2) * HALF + z // 2
    return jnp.where(dst == col, 1.0, 0.0).astype(BF)


class Net:
    def __init__(self, out_sem):
        self.out_sem, self.count, self.started = out_sem, 0, []

    def go(self, src, dst, in_sem, device, cond=None):
        copy = send(src, dst, self.out_sem.at[self.count], in_sem, device)
        self.count += 1
        self.started.append((copy, cond))
        if cond is None:
            copy.start()
        else:
            pl.when(cond)(copy.start)

    def wait(self, dst, in_sem, device, cond=None):
        copy = send(dst, dst, self.out_sem.at[0], in_sem, device)
        if cond is None:
            copy.wait_recv()
        else:
            pl.when(cond)(copy.wait_recv)

    def drain(self):
        for copy, cond in self.started:
            if cond is None:
                copy.wait_send()
            else:
                pl.when(cond)(copy.wait_send)


SENDS = 160


def layer_kernel(
    sizes, width, scale, v_hbm, w_hbm, b_ref, g_hbm,
    act_ref, gx_ref, dwb_ref, d8_ref, db_ref,
    v_ref, g_ref, w2, xg, xb, x8, acc, carry, dysh, dyt, gx_far, gx_in, gx_own,
    out_sem, local_sem, g_in, b_in, e_in, e_all, dy_in, dyt_in, dw_in, gx_sem, misc_in,
):
    n_dp, n_space, n_chan = sizes
    blocks = n_dp * n_space
    y, z, c = place()
    chip, core = c // 2, c % 2
    b = y * n_space + z
    twin = (y, z, 2 * chip + 1 - core)
    far = (y, z, 2 * (1 - chip) + core)
    cf = 2 * (1 - chip) + core
    right = (y, jnp.minimum(z + 1, n_space - 1), c)
    left = (y, jnp.maximum(z - 1, 0), c)
    across = (1 - y, z, c)
    net = Net(out_sem)

    own_v = pltpu.make_async_copy(v_hbm, v_ref, local_sem.at[3])
    own_v.start()
    own_g = pltpu.make_async_copy(g_hbm, g_ref, local_sem.at[4])
    own_g.start()
    barrier = pltpu.get_barrier_semaphore()
    for device in (twin, far):
        pl.semaphore_signal(barrier, 1, device_id=device, device_id_type=pl.DeviceIdType.MESH)
    for o in range(1, blocks):
        h = (b + o) % blocks
        pl.semaphore_signal(
            barrier, 1, device_id=(h // n_space, h % n_space, c), device_id_type=pl.DeviceIdType.MESH
        )
    own_w = pltpu.make_async_copy(w_hbm, w2.at[0], local_sem.at[0])
    own_w.start()

    part = v_ref.shape[1]
    half = CELLS // 2
    parity = parity_block()
    own_v.wait()
    for h in range(2):
        r = jnp.dot(
            v_ref[:, :, 2 * CELLS * h : 2 * CELLS * (h + 1)].reshape(2 * part, 2 * CELLS), parity,
            preferred_element_type=F32,
        ).astype(BF)
        for k, (p, ph) in enumerate(ORDER):
            tile = r[p * part : (p + 1) * part, ph * half : (ph + 1) * half]
            xg[c, k, :, h * half : (h + 1) * half] = tile
            if k == EIGHT:
                x8[c, b, :, h * half : (h + 1) * half] = tile

    pl.semaphore_wait(barrier, blocks + 1)

    spans = [pl.ds(0, EARLY), pl.ds(EARLY, 8 - EARLY)]
    for m in range(2):
        block = xg.at[c, spans[m]]
        net.go(block, block, g_in.at[m, c], far)
        net.go(block, block, g_in.at[m, c], twin)

    def chain_start(ref, sem):
        net.go(ref, ref, sem, right, z < n_space - 1)
        net.go(ref, ref, sem, left, z > 0)
        net.go(ref, ref, sem, across)

    def chain_step(d, ref_of, sem_of):
        for ok, zz, on, onward in (
            (z - d >= 0, jnp.maximum(z - d, 0), right, z < n_space - 1),
            (z + d < n_space, jnp.minimum(z + d, n_space - 1), left, z > 0),
        ):
            s = y * n_space + zz
            net.wait(ref_of(s), sem_of(s), left, ok)
            if d < n_space - 1:
                net.go(ref_of(s), ref_of(s), sem_of(s), on, ok & onward)
            net.go(ref_of(s), ref_of(s), sem_of(s), across, ok)

    def chain_end(zz, ref_of, sem_of, then=None):
        s = (1 - y) * n_space + zz
        net.wait(ref_of(s), sem_of(s), across)
        if then is not None:
            then(s)

    def row_start(ref, sem):
        for o in range(1, n_space):
            net.go(ref, ref, sem, (y, (z + o) % n_space, c))
        net.go(ref, ref, sem, across)

    def row_step(o, ref_of, sem_of, then=None):
        s = y * n_space + (z + o) % n_space
        net.wait(ref_of(s), sem_of(s), left)
        net.go(ref_of(s), ref_of(s), sem_of(s), across)
        if then is not None:
            then(s)

    rows = part // 2
    for row in range(n_dp):
        for zl in range(2):
            to = (row, 2 * core + zl, c)
            net.go(
                xg.at[c, pl.ds(4 * row, 4), pl.ds(rows * zl, rows)], xb.at[chip, b], b_in.at[chip, b], to,
                jnp.logical_not((y == row) & (z == 2 * core + zl)),
            )

    def eight(s):
        return x8.at[c, s]

    def eight_sem(s):
        return e_in.at[s]

    row_start(x8.at[c, b], e_in.at[b])
    net.go(w_hbm, w2.at[1], misc_in.at[0], twin)
    own_w.wait()
    own_g.wait()

    def columns(t, first, count):
        return pl.ds(pl.multiple_of(t * width + first * part, 128), count * part)

    def forward_part(ch, ready, group, s, first):
        total = None if first else acc[4 * group + s]
        for t, tap in enumerate(TAPS):
            k = class_of(tap)
            if shift_of(tap[1], tap[2]) != s or (tap[0] == 0) != (group == 0) or k not in ready:
                continue
            term = jnp.dot(
                w2[0, :, columns(t, 2 * ch, 2)],
                xg[pl.ds(2 * ch, 2), k].reshape(2 * part, CELLS),
                preferred_element_type=F32,
            )
            total = term if total is None else total + term
        acc[4 * group + s] = total

    for m in range(2):
        net.wait(xg.at[twin[2], spans[m]], g_in.at[m, twin[2]], twin)
    relay = core == z // 2

    def relay_share(o):
        s = (b + o) % blocks
        net.wait(xb.at[chip, s], b_in.at[chip, s], across, relay)
        net.go(xb.at[chip, s], xb.at[chip, s], b_in.at[chip, s], far, relay)
        net.go(xb.at[chip, s], xb.at[chip, s], b_in.at[chip, s], twin, relay)

    for s in range(4):
        for group in range(2):
            forward_part(chip, range(8), group, s, True)
    early, late = range(EARLY), range(EARLY, 8)
    other = 2 * (1 - chip) + 1 - core

    def far_arrived(m):
        net.wait(xg.at[cf, spans[m]], g_in.at[m, cf], far)
        net.go(xg.at[cf, spans[m]], xg.at[cf, spans[m]], g_in.at[m, cf], twin)
        net.wait(xg.at[other, spans[m]], g_in.at[m, other], twin)

    far_arrived(0)
    for s in range(4):
        forward_part(1 - chip, early, 0, s, False)
    ahead = acc[0]
    for s in (1, 2, 3):
        ahead = ahead + forward_shift(acc[s], s)
    carry[0] = ahead
    net.go(carry.at[0], carry.at[1], misc_in.at[1], right, z < n_space - 1)
    for s in range(4):
        forward_part(1 - chip, early, 1, s, False)
    far_arrived(1)
    for o in range(1, blocks):
        relay_share(o)

    for s in range(4):
        forward_part(1 - chip, late, 1, s, False)
    diagonal = lax.broadcasted_iota(jnp.int32, (part, part), 0) == lax.broadcasted_iota(jnp.int32, (part, part), 1)
    u = jnp.sum(jnp.where(diagonal, b_ref[...], 0.0), axis=1, keepdims=True) + acc[4]
    for s in (1, 2, 3):
        u = u + forward_shift(acc[4 + s], s)

    @pl.when(z == 0)
    def _():
        carry[1] = jnp.zeros_like(carry[1])

    net.wait(carry.at[1], misc_in.at[1], left, z > 0)
    u = u + carry[1]
    k0 = 0.7978845608028654
    th = jnp.tanh(k0 * (u + 0.044715 * (u * u * u)))
    slope = 0.5 * (1.0 + th) + 0.5 * u * (1.0 - th * th) * k0 * (1.0 + 3 * 0.044715 * u * u)
    dysh[0, b] = (g_ref[...].astype(F32) * slope).astype(BF)
    act_ref[...] = (0.5 * u * (1.0 + th)).astype(BF)

    def dy_of(s):
        return dysh.at[0, s]

    def dy_sem(s):
        return dy_in.at[s]

    row_start(dysh.at[0, b], dy_in.at[b])
    net.go(dysh.at[0, b], dyt.at[0, 0], dyt_in.at[0], twin)
    own_slots = []
    for hx in range(2):
        own_slots.append(
            pltpu.make_async_copy(
                xg.at[2 * hx + z // 2, pl.ds(4 * y, 4), pl.ds(pl.multiple_of(rows * (z % 2), rows), rows)],
                xb.at[hx, b],
                local_sem.at[1 + hx],
            )
        )
        own_slots[-1].start()

    def shift_slot(s):
        wide = dysh[0, s].astype(F32)
        for k in (1, 2, 3):
            dysh[k, s] = backward_shift(wide, k).astype(BF)

    for o in range(1, n_space):
        row_step(o, eight, eight_sem)
    shift_slot(b)
    for o in (1, 3, 2):
        row_step(o, dy_of, dy_sem)
    nxt = y * n_space + jnp.minimum(z + 1, n_space - 1)
    net.go(dysh.at[0, nxt], dyt.at[0, 1], dyt_in.at[1], twin, z < n_space - 1)
    for o in range(1, n_space):
        shift_slot(y * n_space + (z + o) % n_space)
    for zz in range(n_space):
        chain_end(zz, eight, eight_sem)

    for r in range(n_dp):
        mine = x8.at[c, pl.ds(n_space * r, n_space)]
        net.go(mine, mine, e_all.at[r, c], far)
        net.go(mine, mine, e_all.at[r, c], twin)
    for o in (0, 1, 3, 2):
        chain_end((z + o) % n_space, dy_of, dy_sem, shift_slot)

    for o in range(1, blocks):
        s = (b + o) % blocks
        net.wait(xb.at[chip, s], b_in.at[chip, s], twin, jnp.logical_not(relay))
    for copy in own_slots:
        copy.wait()

    def share_half(row, i, side):
        _, (k1, k2, k3), k = share_taps(row)[i]
        total = None
        for v in range(n_dp):
            for zz in range(n_space - (k1 == 0)):
                s = v * n_space + zz
                term = lax.dot_general(
                    dysh[shift_of(k2, k3), s + (k1 == 0)], xb[side, s, k], NT, preferred_element_type=F32
                )
                total = term if total is None else total + term
        return total * scale

    def share_piece(row, i, side):
        first = 2 * (i % (PIECES // 2))
        low = share_half(row, first, side)
        high = share_half(row, first + 1, side) if first + 1 < len(share_taps(row)) else jnp.zeros_like(low)
        dwb_ref[b, i] = jnp.concatenate([low, high], axis=1).astype(BF)

    def dw_of(m):
        lo, hi = CHUNKS[m]
        return lambda s: dwb_ref.at[s, pl.ds(lo, hi - lo)]

    def dw_sem(m):
        return lambda s: dw_in.at[m, s]

    def share_chunk(m):
        lo, hi = CHUNKS[m]
        for row in range(n_dp):
            @pl.when(y == row)
            def _():
                for i in range(lo, hi):
                    share_piece(row, i, chip if i < PIECES // 2 else 1 - chip)
        chain_start(dw_of(m)(b), dw_sem(m)(b))

    for m in (0, 1):
        share_chunk(m)
    for o in range(1, blocks):
        s = (b + o) % blocks
        other_half = xb.at[1 - chip, s]
        net.wait(other_half, b_in.at[1 - chip, s], far, relay)
        net.go(other_half, other_half, b_in.at[1 - chip, s], twin, relay)
    for o in range(1, blocks):
        s = (b + o) % blocks
        net.wait(xb.at[1 - chip, s], b_in.at[1 - chip, s], twin, jnp.logical_not(relay))
    for m in (2, 3):
        share_chunk(m)

    @pl.when(z == n_space - 1)
    def _():
        dyt[0, 1] = jnp.zeros_like(dyt[0, 1])

    net.wait(dyt.at[0, 0], dyt_in.at[0], twin)
    net.wait(dyt.at[0, 1], dyt_in.at[1], twin, z < n_space - 1)
    for i in range(2):
        wide = dyt[0, i].astype(F32)
        for k in (1, 2, 3):
            dyt[k, i] = backward_shift(wide, k).astype(BF)
    net.wait(w2.at[1], misc_in.at[0], twin)
    edge = jnp.where(z < n_space - 1, 1.0, 0.0).astype(BF)

    def input_grad(j, p, ph):
        total = None
        for t, (k1, k2, k3) in enumerate(TAPS):
            if phase_of(k2, k3) != ph or (k1 != 1) != (p == 1):
                continue
            s = shift_of(k2, k3)
            here = dysh[s, nxt] * edge if k1 == 0 else dysh[s, b]
            for i, view in enumerate((here, dyt[s, int(k1 == 0)])):
                term = lax.dot_general(
                    w2[i, :, columns(t, j, 1)], view, TN, preferred_element_type=F32
                )
                total = term if total is None else total + term
        return total

    for p in range(2):
        for ph in range(4):
            gx_far[p, ph] = input_grad(cf, p, ph).astype(BF)
        net.go(gx_far.at[p], gx_in.at[p], gx_sem.at[p], far)

    def pass_on(d, *chunks):
        for m in chunks:
            chain_step(d, dw_of(m), dw_sem(m))

    pass_on(1, 0, 1)
    for ph in range(4):
        gx_own[0, ph] = input_grad(c, 0, ph)
    pass_on(1, 2, 3)
    for ph in range(4):
        gx_own[1, ph] = input_grad(c, 1, ph)
    pass_on(2, 0, 1)

    for r in range(n_dp):
        theirs = x8.at[cf, pl.ds(n_space * r, n_space)]
        net.wait(theirs, e_all.at[r, cf], far)
        net.go(theirs, theirs, e_all.at[r, cf], twin)
    pass_on(2, 2, 3)
    for r in range(n_dp):
        for j in (twin[2], other):
            net.wait(x8.at[j, pl.ds(n_space * r, n_space)], e_all.at[r, j], twin)
    for k in range(2):
        for v in range(n_dp):
            for zz in range(n_space - (k == 0)):
                s = v * n_space + zz
                term = lax.dot_general(
                    dysh[:, s + (k == 0)].reshape(4 * part, CELLS),
                    x8[:, s].reshape(n_chan * part, CELLS),
                    NT,
                    preferred_element_type=F32,
                ) * scale
                if s == 0:
                    d8_ref[k] = term
                else:
                    d8_ref[k] += term
        pass_on(3, *((0, 1) if k == 0 else (2, 3)))
    ones = jnp.ones((8, CELLS), BF)
    total = None
    for s in range(blocks):
        term = lax.dot_general(ones, dysh[0, s], NT, preferred_element_type=F32)
        total = term if total is None else total + term
    db_ref[...] = total * scale

    for p in range(2):
        net.wait(gx_in.at[p], gx_sem.at[p], far)
    for p in range(2):
        cells = [(gx_own[p, ph] + gx_in[p, ph].astype(F32)).astype(BF) for ph in range(4)]
        for h in range(2):
            strip = jnp.concatenate([cell[:, h * half : (h + 1) * half] for cell in cells], axis=1)
            gx_ref[p, :, 2 * CELLS * h : 2 * CELLS * (h + 1)] = lax.dot_general(
                strip, parity_block(), NT, preferred_element_type=F32
            ).astype(BF)
    for m in range(len(CHUNKS)):
        for zz in range(n_space):
            chain_end(zz, dw_of(m), dw_sem(m))
    net.drain()


def finish_kernel(n_space, part, dwb_ref, d8_ref, gx_ref, act_ref, db_ref, act_out, gx_out, dw_out, db_out, wide, sem):
    chip = lax.axis_index("chan") // 2
    copies = [
        pltpu.make_async_copy(gx_ref, gx_out, sem.at[len(TAPS)]),
        pltpu.make_async_copy(act_ref, act_out, sem.at[len(TAPS) + 1]),
    ]
    for copy in copies:
        copy.start()
    db_out[...] = db_ref[0:1]
    width = 4 * part
    where = {}
    for row in range(2):
        for i, (t, _, _) in enumerate(share_taps(row)):
            where[t] = (row, i)
    low = lax.broadcasted_iota(jnp.int32, (part, part), 1) < part // 2
    for t, (k1, k2, k3) in enumerate(TAPS):
        first = t * width
        if t in where:
            row, i = where[t]
            for j in range(4):
                q = i // 2 + PIECES // 2 * jnp.where(chip == j // 2, 0, 1)
                even = dwb_ref[row * n_space + 2 * (j % 2), q].astype(F32)
                odd = dwb_ref[row * n_space + 2 * (j % 2) + 1, q].astype(F32)
                if i % 2:
                    even = pltpu.roll(even, part // 2, 1)
                else:
                    odd = pltpu.roll(odd, part // 2, 1)
                wide[:, first + j * part : first + (j + 1) * part] = jnp.where(low, even, odd)
        else:
            s = shift_of(k2, k3)
            wide[:, first : first + width] = d8_ref[int(k1 == 2), s * part : (s + 1) * part]
        span = pl.ds(first, width)
        copies.append(pltpu.make_async_copy(wide.at[:, span], dw_out.at[:, span], sem.at[t]))
        copies[-1].start()
    for copy in copies:
        copy.wait()


def per_device_shared(volumes, kernel, bias, act_grad):
    batch, planes, part, cells = volumes.shape
    filters = kernel.shape[0]
    width = kernel.shape[1] // 27
    sizes = tuple(lax.axis_size(a) for a in ("dp", "space", "chan"))
    n_dp, n_space, n_chan = sizes
    blocks = n_dp * n_space
    dma = pltpu.SemaphoreType.DMA
    flops = 2 * 27 * width * filters * CELLS
    ANY = pl.BlockSpec(memory_space=pl.ANY)
    act, gx, dwb, d8, db = pl.pallas_call(
        functools.partial(layer_kernel, sizes, width, 1.0 / (batch * n_dp)),
        out_shape=(
            shape(filters, CELLS),
            shape(planes, part, cells),
            shape(blocks, PIECES, filters, part),
            shape(2, 4 * filters, width, dtype=F32),
            shape(8, filters, dtype=F32),
        ),
        in_specs=[ANY, ANY, VM, ANY],
        out_specs=[VM] * 5,
        scratch_shapes=(
            pltpu.VMEM((planes, part, cells), BF),
            pltpu.VMEM((filters, CELLS), BF),
            pltpu.VMEM((2, filters, 27 * width), BF),
            pltpu.VMEM((n_chan, 8, part, CELLS), BF),
            pltpu.VMEM((2, blocks, 4, part // 2, CELLS), BF),
            pltpu.VMEM((n_chan, blocks, part, CELLS), BF),
            pltpu.VMEM((8, filters, CELLS), F32),
            pltpu.VMEM((2, filters, CELLS), F32),
            pltpu.VMEM((4, blocks, filters, CELLS), BF),
            pltpu.VMEM((4, 2, filters, CELLS), BF),
            pltpu.VMEM((2, 4, part, CELLS), BF),
            pltpu.VMEM((2, 4, part, CELLS), BF),
            pltpu.VMEM((2, 4, part, CELLS), F32),
            dma((SENDS,)),
            dma((5,)),
            dma((2, n_chan)),
            dma((2, blocks)),
            dma((blocks,)),
            dma((n_dp, n_chan)),
            dma((blocks,)),
            dma((2,)),
            dma((len(CHUNKS), blocks)),
            dma((2,)),
            dma((2,)),
        ),
        compiler_params=pltpu.CompilerParams(
            vmem_limit_bytes=46 << 20, collective_id=0, has_side_effects=True
        ),
        cost_estimate=pl.CostEstimate(flops=5 * flops, bytes_accessed=12 << 20, transcendentals=0),
    )(volumes.reshape(planes, part, cells), kernel, bias.reshape(1, filters), act_grad.reshape(filters, CELLS))
    act, gx, dw, db = pl.pallas_call(
        functools.partial(finish_kernel, n_space, part),
        out_shape=(
            shape(filters, CELLS),
            shape(planes, part, cells),
            shape(filters, 27 * width, dtype=F32),
            shape(1, filters, dtype=F32),
        ),
        in_specs=[VM] * 5,
        out_specs=[ANY, ANY, ANY, VM],
        scratch_shapes=(pltpu.VMEM((filters, 27 * width), F32), dma((len(TAPS) + 2,))),
        compiler_params=pltpu.CompilerParams(vmem_limit_bytes=40 << 20),
        cost_estimate=pl.CostEstimate(flops=0, bytes_accessed=12 << 20, transcendentals=0),
    )(dwb, d8, gx, act, db)
    return act.reshape(act_grad.shape), gx.reshape(volumes.shape), dw, db.reshape(filters)


def solution(mesh):
    shared = (mesh.shape["dp"], mesh.shape["space"], mesh.shape["chan"]) == (2, 4, 4)
    in_specs = (
        P("dp", "space", "chan", None),
        P("chan", None),
        P("chan"),
        P("dp", "space", "chan", None),
    )
    out_specs = (
        P("dp", "space", "chan", None),
        P("dp", "space", "chan", None),
        P("chan", None),
        P("chan"),
    )
    return jax.shard_map(
        per_device_shared if shared else per_device,
        mesh=mesh, in_specs=in_specs, out_specs=out_specs, check_vma=False,
    )
```

```python
import functools

import jax
import jax.numpy as jnp
from jax import lax
from jax.experimental import pallas as pl
from jax.experimental.pallas import tpu as pltpu
from jax.sharding import PartitionSpec as P

GRID = 32
HALF = GRID // 2
CELLS = HALF * HALF
BF = jnp.bfloat16
F32 = jnp.float32
VM = pl.BlockSpec(memory_space=pltpu.VMEM)
TAPS = [(k1, k2, k3) for k1 in range(3) for k2 in range(3) for k3 in range(3)]


def phase_of(k2, k3):
    return 2 * (k2 != 1) + (k3 != 1)


def shift_of(k2, k3):
    return 2 * (k2 == 0) + (k3 == 0)


def parity_matrix():
    full = GRID * GRID
    dst = lax.broadcasted_iota(jnp.int32, (1, full), 1)
    phase, cell = dst // CELLS, dst % CELLS
    y = 2 * (cell // HALF) + phase // 2
    z = 2 * (cell % HALF) + phase % 2
    src = y * GRID + z
    rows = lax.broadcasted_iota(jnp.int32, (full, full), 0)
    return jnp.where(rows == src, 1.0, 0.0).astype(BF)


def lanes():
    return lax.broadcasted_iota(jnp.int32, (1, CELLS), 1)


def forward_shift(x, s):
    if s & 2:
        x = jnp.where(lanes() >= HALF, pltpu.roll(x, HALF, 1), 0.0)
    if s & 1:
        x = jnp.where(lanes() % HALF != 0, pltpu.roll(x, 1, 1), 0.0)
    return x


def backward_shift(x, s):
    if s & 2:
        x = jnp.where(lanes() < CELLS - HALF, pltpu.roll(x, CELLS - HALF, 1), 0.0)
    if s & 1:
        x = jnp.where(lanes() % HALF != HALF - 1, pltpu.roll(x, CELLS - 1, 1), 0.0)
    return x


def split_kernel(v_ref, p_ref, o_ref):
    o_ref[...] = jnp.dot(v_ref[...], p_ref[...], preferred_element_type=F32).astype(BF)


def merge_kernel(v_ref, p_ref, o_ref):
    total = v_ref[0].astype(F32)
    for j in range(1, v_ref.shape[0]):
        total = total + v_ref[j].astype(F32)
    o_ref[...] = lax.dot_general(
        total.astype(BF).reshape(o_ref.shape), p_ref[...], (((1,), (1,)), ((), ())), preferred_element_type=F32
    ).astype(BF)


def send(src, dst, send_sem, recv_sem, device):
    return pltpu.make_async_remote_copy(
        src, dst, send_sem, recv_sem, device_id=device, device_id_type=pl.DeviceIdType.MESH
    )


def place():
    return lax.axis_index("dp"), lax.axis_index("space"), lax.axis_index("chan")


def greet(sizes):
    n_dp, n_space, n_chan = sizes
    y, z, c = place()
    barrier = pltpu.get_barrier_semaphore()
    g = y * n_space + z
    for o in range(1, n_chan):
        pl.semaphore_signal(
            barrier, 1, device_id=(y, z, (c + o) % n_chan), device_id_type=pl.DeviceIdType.MESH
        )
    for o in range(1, n_dp * n_space):
        h = (g + o) % (n_dp * n_space)
        pl.semaphore_signal(
            barrier, 1, device_id=(h // n_space, h % n_space, c), device_id_type=pl.DeviceIdType.MESH
        )
    pl.semaphore_wait(barrier, n_chan + n_dp * n_space - 2)


def gather_inputs(sizes, own_ref, x_ref, out_sem, in_sem, local_sem):
    n_dp, n_space, n_chan = sizes
    chips = n_chan // 2
    y, z, c = place()
    chip, core = c // 2, c % 2
    twin = (y, z, 2 * chip + 1 - core)
    greet(sizes)

    def planes(k):
        return pl.ds(1, 2) if k else pl.ds(0, 1)

    def block(k, j):
        return x_ref.at[planes(k), j]

    def to_chip(k, o, src):
        return send(
            src, block(k, c), out_sem.at[k, 0, o], in_sem.at[k, c],
            (y, z, 2 * ((chip + o) % chips) + core),
        )

    def to_twin(k, o, src):
        j = 2 * ((chip - o + chips) % chips) + core
        return send(src, block(k, j), out_sem.at[k, 1, o], in_sem.at[k, j], twin)

    def arrived(k, j):
        send(block(k, j), block(k, j), out_sem.at[k, 1, 0], in_sem.at[k, j], twin).wait_recv()

    rim = send(own_ref.at[pl.ds(1, 1)], block(0, c), out_sem.at[0, 2, 0], in_sem.at[0, c], (y, jnp.minimum(z + 1, n_space - 1), c))
    sends = [to_chip(1, o, own_ref) for o in range(1, chips)] + [to_twin(1, 0, own_ref)]

    @pl.when(z < n_space - 1)
    def _():
        rim.start()

    for copy in sends:
        copy.start()
    keep = pltpu.make_async_copy(own_ref, block(1, c), local_sem)
    keep.start()

    rim_out = [to_chip(0, o, block(0, c)) for o in range(1, chips)] + [to_twin(0, 0, block(0, c))]

    @pl.when(z > 0)
    def _():
        arrived(0, c)
        for copy in rim_out:
            copy.start()

    @pl.when(z == 0)
    def _():
        x_ref[0] = jnp.zeros_like(x_ref[0])

    for o in range(1, chips):
        j = 2 * ((chip - o + chips) % chips) + core
        arrived(1, j)
        passed = to_twin(1, o, block(1, j))
        passed.start()
        sends.append(passed)

    @pl.when(z > 0)
    def _():
        for o in range(1, chips):
            j = 2 * ((chip - o + chips) % chips) + core
            arrived(0, j)
            passed = to_twin(0, o, block(0, j))
            passed.start()
            rim_out.append(passed)
        for o in range(chips):
            arrived(0, 2 * ((chip - o + chips) % chips) + 1 - core)
        for copy in rim_out:
            copy.wait_send()

    for o in range(chips):
        arrived(1, 2 * ((chip - o + chips) % chips) + 1 - core)
    for copy in sends:
        copy.wait_send()

    @pl.when(z < n_space - 1)
    def _():
        rim.wait_send()

    keep.wait()


def forward_kernel(
    sizes, width, own_ref, w_ref, b_ref, g_ref, x_ref, act_ref, dy_ref, db_ref, out_sem, in_sem, local_sem
):
    gather_inputs(sizes, own_ref, x_ref, out_sem, in_sem, local_sem)
    sums = [None] * 4
    for t, (k1, k2, k3) in enumerate(TAPS):
        ph, s = phase_of(k2, k3), shift_of(k2, k3)
        part = jnp.dot(
            w_ref[:, t * width : (t + 1) * width],
            x_ref[k1, :, :, ph * CELLS : (ph + 1) * CELLS].reshape(width, CELLS),
            preferred_element_type=F32,
        )
        sums[s] = part if sums[s] is None else sums[s] + part
    u = b_ref[...] + sums[0]
    for s in (1, 2, 3):
        u = u + forward_shift(sums[s], s)
    c = 0.7978845608028654
    th = jnp.tanh(c * (u + 0.044715 * (u * u * u)))
    act_ref[...] = (0.5 * u * (1.0 + th)).astype(BF)
    slope = 0.5 * (1.0 + th) + 0.5 * u * (1.0 - th * th) * c * (1.0 + 3 * 0.044715 * u * u)
    dy = (g_ref[...].astype(F32) * slope).astype(BF)
    dy_ref[...] = dy
    db_ref[...] = lax.dot_general(
        jnp.ones((8, CELLS), BF), dy, (((1,), (1,)), ((), ())), preferred_element_type=F32
    )


def shifted(dy):
    wide = dy.astype(F32)
    return [dy] + [backward_shift(wide, s).astype(BF) for s in (1, 2, 3)]


def grads_kernel(sizes, width, x_ref, w_ref, dy_ref, dw_ref, gx_ref, next_ref, out_sem, in_sem):
    n_space = sizes[1]
    y, z, c = place()
    greet(sizes)
    back = send(dy_ref, next_ref, out_sem, in_sem, (y, jnp.maximum(z - 1, 0), c))

    @pl.when(z > 0)
    def _():
        back.start()

    own = shifted(dy_ref[...])
    for t, (k1, k2, k3) in enumerate(TAPS):
        ph, s = phase_of(k2, k3), shift_of(k2, k3)
        part = lax.dot_general(
            own[s],
            x_ref[k1, :, :, ph * CELLS : (ph + 1) * CELLS].reshape(width, CELLS),
            (((1,), (1,)), ((), ())),
            preferred_element_type=F32,
        )
        dw_ref[:, t * width : (t + 1) * width] = part.astype(BF)

    @pl.when(z < n_space - 1)
    def _():
        back.wait_recv()

    @pl.when(z == n_space - 1)
    def _():
        next_ref[...] = jnp.zeros_like(next_ref)

    following = shifted(next_ref[...])
    for plane in range(2):
        for ph in range(4):
            total = None
            for t, (k1, k2, k3) in enumerate(TAPS):
                if phase_of(k2, k3) != ph or (k1 == 1) != (plane == 0):
                    continue
                views = following if k1 == 0 else own
                part = lax.dot_general(
                    w_ref[:, t * width : (t + 1) * width],
                    views[shift_of(k2, k3)],
                    (((0,), (0,)), ((), ())),
                    preferred_element_type=F32,
                )
                total = part if total is None else total + part
            gx_ref[:, plane, :, ph * CELLS : (ph + 1) * CELLS] = total.astype(BF).reshape(
                gx_ref.shape[0], gx_ref.shape[2], CELLS
            )

    @pl.when(z > 0)
    def _():
        back.wait_send()


def share_kernel(
    sizes, dw_ref, gx_ref, db_ref, all_ref, parts_ref, dbs_ref, y_ref, r_ref, l_ref, s_ref,
    out_sem, in_sem, gx_out, gx_in, db_out, db_in, local_sem, y_out, y_in, z_out, r_in, l_in
):
    n_dp, n_space, n_chan = sizes
    group = n_dp * n_space
    y, z, c = place()
    g = y * n_space + z
    greet(sizes)
    right = (y, jnp.minimum(z + 1, n_space - 1), c)
    left = (y, jnp.maximum(z - 1, 0), c)
    across = (1 - y, z, c)

    def hop(way, device, j, src=None):
        slot = all_ref.at[y * n_space + j]
        return send(slot if src is None else src, slot, out_sem.at[way, j], in_sem.at[y * n_space + j], device)

    def arrived(h):
        send(all_ref.at[h], all_ref.at[h], out_sem.at[2, 0], in_sem.at[h], across).wait_recv()

    locals_ = [
        pltpu.make_async_copy(gx_ref.at[c], parts_ref.at[c], local_sem.at[1]),
        pltpu.make_async_copy(db_ref, dbs_ref.at[g], local_sem.at[2]),
    ]

    def over(j):
        return send(dw_ref.at[(1 - y) * n_space + j], y_ref.at[j], y_out.at[j], y_in.at[j], across)

    def rightward(j):
        return send(s_ref.at[j], r_ref.at[j], z_out.at[j], r_in.at[j], right)

    def leftward(j):
        return send(s_ref.at[j], l_ref.at[j], z_out.at[j], l_in.at[j], left)

    def both(j):
        over(j).wait_recv()
        return dw_ref[y * n_space + j].astype(F32) + y_ref[j].astype(F32)

    for d in range(n_space - 1, 0, -1):
        @pl.when(z + d < n_space)
        def _():
            over(jnp.minimum(z + d, n_space - 1)).start()

        @pl.when(z - d >= 0)
        def _():
            over(jnp.maximum(z - d, 0)).start()

    over(z).start()
    extra = []
    for o in range(1, n_chan):
        to = (c + o) % n_chan
        extra.append(
            send(gx_ref.at[to], parts_ref.at[c], gx_out.at[o], gx_in.at[o], (y, z, to))
        )
    for o in range(1, group):
        to = (g + o) % group
        extra.append(
            send(db_ref, dbs_ref.at[g], db_out.at[o], db_in.at[o], (to // n_space, to % n_space, c))
        )
    for copy in extra:
        copy.start()
    for copy in locals_:
        copy.start()

    for d in range(n_space - 1, 0, -1):
        @pl.when(z + d < n_space)
        def _():
            j = jnp.minimum(z + d, n_space - 1)
            mine = both(j)

            @pl.when(z == 0)
            def _():
                s_ref[j] = mine.astype(BF)

            @pl.when(z > 0)
            def _():
                rightward(j).wait_recv()
                s_ref[j] = (mine + r_ref[j].astype(F32)).astype(BF)

            rightward(j).start()

        @pl.when(z - d >= 0)
        def _():
            j = jnp.maximum(z - d, 0)
            mine = both(j)

            @pl.when(z == n_space - 1)
            def _():
                s_ref[j] = mine.astype(BF)

            @pl.when(z < n_space - 1)
            def _():
                leftward(j).wait_recv()
                s_ref[j] = (mine + l_ref[j].astype(F32)).astype(BF)

            leftward(j).start()

    @pl.when(z == 0)
    def _():
        r_ref[z] = jnp.zeros_like(r_ref[z])

    @pl.when(z == n_space - 1)
    def _():
        l_ref[z] = jnp.zeros_like(l_ref[z])

    @pl.when(z > 0)
    def _():
        rightward(z).wait_recv()

    @pl.when(z < n_space - 1)
    def _():
        leftward(z).wait_recv()

    all_ref[g] = (both(z) + r_ref[z].astype(F32) + l_ref[z].astype(F32)).astype(BF)

    @pl.when(z < n_space - 1)
    def _():
        hop(0, right, z).start()

    @pl.when(z > 0)
    def _():
        hop(1, left, z).start()

    hop(2, across, z).start()

    for d in range(1, n_space):
        @pl.when(z - d >= 0)
        def _():
            j = jnp.maximum(z - d, 0)
            arrived(y * n_space + j)

            @pl.when(z < n_space - 1)
            def _():
                hop(0, right, j).start()

            hop(2, across, j).start()

        @pl.when(z + d < n_space)
        def _():
            j = jnp.minimum(z + d, n_space - 1)
            arrived(y * n_space + j)

            @pl.when(z > 0)
            def _():
                hop(1, left, j).start()

            hop(2, across, j).start()

    for o in range(1, n_chan):
        frm = (c - o + n_chan) % n_chan
        send(parts_ref.at[frm], parts_ref.at[frm], gx_out.at[o], gx_in.at[o], (y, z, frm)).wait_recv()
    for o in range(1, group):
        frm = (g - o + group) % group
        send(dbs_ref.at[frm], dbs_ref.at[frm], db_out.at[o], db_in.at[o], (frm // n_space, frm % n_space, c)).wait_recv()
    for j in range(n_space):
        arrived((1 - y) * n_space + j)
        hop(2, across, j).wait_send()

        @pl.when((j <= z) & (z < n_space - 1))
        def _():
            hop(0, right, j).wait_send()

        @pl.when((j >= z) & (z > 0))
        def _():
            hop(1, left, j).wait_send()

        over(j).wait_send()

        @pl.when(j > z)
        def _():
            rightward(j).wait_send()

        @pl.when(j < z)
        def _():
            leftward(j).wait_send()

    for copy in extra:
        copy.wait_send()
    for copy in locals_:
        copy.wait()


def call(kernel, out_shape, n_in, flops, moved, scratch=(), collective_id=None):
    many = isinstance(out_shape, (tuple, list))
    return pl.pallas_call(
        kernel,
        out_shape=out_shape,
        in_specs=[VM] * n_in,
        out_specs=[VM] * len(out_shape) if many else VM,
        scratch_shapes=scratch,
        compiler_params=pltpu.CompilerParams(
            vmem_limit_bytes=48 << 20,
            collective_id=collective_id,
            has_side_effects=collective_id is not None,
        ),
        cost_estimate=pl.CostEstimate(flops=flops, bytes_accessed=moved, transcendentals=0),
    )


def shape(*dims, dtype=BF):
    return jax.ShapeDtypeStruct(dims, dtype)


def per_device(volumes, kernel, bias, act_grad):
    batch, planes, part, cells = volumes.shape
    filters = kernel.shape[0]
    width = kernel.shape[1] // 27
    parity = parity_matrix()
    own = call(split_kernel, shape(planes * part, cells), 2, 2 * planes * part * cells**2, 1 << 20)(
        volumes.reshape(planes * part, cells), parity
    ).reshape(planes, part, cells)
    sizes = tuple(lax.axis_size(a) for a in ("dp", "space", "chan"))
    group, n_chan = sizes[0] * sizes[1], sizes[2]
    dma = pltpu.SemaphoreType.DMA
    flops = 2 * 27 * width * filters * CELLS
    x_all, act, dy, db = call(
        functools.partial(forward_kernel, sizes, width),
        (
            shape(3, n_chan, part, cells),
            shape(filters, CELLS),
            shape(filters, CELLS),
            shape(8, filters, dtype=F32),
        ),
        4,
        flops,
        10 << 20,
        scratch=(dma((2, 3, n_chan // 2)), dma((2, n_chan)), dma),
        collective_id=0,
    )(own, kernel, bias.reshape(filters, 1), act_grad.reshape(filters, CELLS))
    dw, gx = call(
        functools.partial(grads_kernel, sizes, width),
        (shape(filters, 27 * width), shape(n_chan, planes, part, cells)),
        3,
        3 * flops,
        12 << 20,
        scratch=(pltpu.VMEM((filters, CELLS), BF), dma, dma),
        collective_id=2,
    )(x_all, kernel, dy)
    count = batch * sizes[0]
    rows = filters // group
    slots = pltpu.VMEM((sizes[1], rows, 27 * width), BF)
    dw_all, parts, dbs = call(
        functools.partial(share_kernel, sizes),
        (
            shape(group, rows, 27 * width),
            shape(n_chan, planes, part, cells),
            shape(group, 8, filters, dtype=F32),
        ),
        3,
        0,
        12 << 20,
        scratch=(
            slots,
            slots,
            slots,
            slots,
            dma((3, sizes[1])),
            dma((group,)),
            dma((n_chan,)),
            dma((n_chan,)),
            dma((group,)),
            dma((group,)),
            dma((3,)),
            dma((sizes[1],)),
            dma((sizes[1],)),
            dma((sizes[1],)),
            dma((sizes[1],)),
            dma((sizes[1],)),
        ),
        collective_id=1,
    )(dw.reshape(group, rows, 27 * width), gx, db)
    grad_w = dw_all.reshape(filters, 27 * width).astype(F32) / count
    grad_b = jnp.sum(dbs[:, 0], axis=0) / count
    grad_x = call(merge_kernel, shape(planes * part, cells), 2, 2 * planes * part * cells**2, 1 << 20)(
        parts, parity
    )
    return (
        act.reshape(act_grad.shape),
        grad_x.reshape(volumes.shape),
        grad_w,
        grad_b,
    )


ORDER = [(0, 1), (1, 1), (1, 2), (1, 3), (1, 0), (0, 0), (0, 2), (0, 3)]
EIGHT = ORDER.index((1, 3))
EARLY = 5
SHARE = (3, 4)
PIECES = 10
CHUNKS = [(0, 2), (2, 5), (5, 7), (7, 10)]
NT = (((1,), (1,)), ((), ()))
TN = (((0,), (0,)), ((), ()))


def class_of(tap):
    return ORDER.index((int(tap[0] != 1), phase_of(tap[1], tap[2])))


def share_taps(row):
    return [
        (t, tap, class_of(tap) - 4 * row)
        for k in range(4 * row, 4 * row + 4)
        for t, tap in enumerate(TAPS)
        if class_of(tap) == k and k != EIGHT
    ]


def parity_block():
    side = 2 * CELLS
    row = lax.broadcasted_iota(jnp.int32, (side, side), 0)
    col = lax.broadcasted_iota(jnp.int32, (side, side), 1)
    y, z = row // GRID, row % GRID
    dst = (2 * (y % 2) + z % 2) * (CELLS // 2) + (y // 2) * HALF + z // 2
    return jnp.where(dst == col, 1.0, 0.0).astype(BF)


class Net:
    def __init__(self, out_sem):
        self.out_sem, self.count, self.started = out_sem, 0, []

    def go(self, src, dst, in_sem, device, cond=None):
        copy = send(src, dst, self.out_sem.at[self.count], in_sem, device)
        self.count += 1
        self.started.append((copy, cond))
        if cond is None:
            copy.start()
        else:
            pl.when(cond)(copy.start)

    def wait(self, dst, in_sem, device, cond=None):
        copy = send(dst, dst, self.out_sem.at[0], in_sem, device)
        if cond is None:
            copy.wait_recv()
        else:
            pl.when(cond)(copy.wait_recv)

    def drain(self):
        for copy, cond in self.started:
            if cond is None:
                copy.wait_send()
            else:
                pl.when(cond)(copy.wait_send)


SENDS = 160


def layer_kernel(
    sizes, width, scale, v_hbm, w_hbm, b_hbm, g_hbm,
    act_ref, gx_ref, dwb_ref, d8_ref, db_ref,
    v_ref, g_ref, b_ref, w2, xg, xb, x8, acc, carry, dysh, dyt, gx_far, gx_in, gx_own,
    out_sem, local_sem, g_in, b_in, e_in, e_all, dy_in, dyt_in, dw_in, gx_sem, misc_in,
):
    n_dp, n_space, n_chan = sizes
    blocks = n_dp * n_space
    y, z, c = place()
    chip, core = c // 2, c % 2
    b = y * n_space + z
    twin = (y, z, 2 * chip + 1 - core)
    far = (y, z, 2 * (1 - chip) + core)
    cf = 2 * (1 - chip) + core
    right = (y, jnp.minimum(z + 1, n_space - 1), c)
    left = (y, jnp.maximum(z - 1, 0), c)
    across = (1 - y, z, c)
    net = Net(out_sem)

    own_v = pltpu.make_async_copy(v_hbm, v_ref, local_sem.at[3])
    own_v.start()
    own_g = pltpu.make_async_copy(g_hbm, g_ref, local_sem.at[4])
    own_g.start()
    own_b = pltpu.make_async_copy(b_hbm, b_ref, local_sem.at[5])
    own_b.start()
    barrier = pltpu.get_barrier_semaphore()
    for device in (twin, far):
        pl.semaphore_signal(barrier, 1, device_id=device, device_id_type=pl.DeviceIdType.MESH)
    for o in range(1, blocks):
        h = (b + o) % blocks
        pl.semaphore_signal(
            barrier, 1, device_id=(h // n_space, h % n_space, c), device_id_type=pl.DeviceIdType.MESH
        )
    own_w = pltpu.make_async_copy(w_hbm, w2.at[0], local_sem.at[0])
    own_w.start()

    part = v_ref.shape[1]
    half = CELLS // 2
    parity = parity_block()
    own_v.wait()
    for h in range(2):
        r = jnp.dot(
            v_ref[:, :, 2 * CELLS * h : 2 * CELLS * (h + 1)].reshape(2 * part, 2 * CELLS), parity,
            preferred_element_type=F32,
        ).astype(BF)
        for k, (p, ph) in enumerate(ORDER):
            tile = r[p * part : (p + 1) * part, ph * half : (ph + 1) * half]
            xg[c, k, :, h * half : (h + 1) * half] = tile
            if k == EIGHT:
                x8[c, b, :, h * half : (h + 1) * half] = tile

    pl.semaphore_wait(barrier, blocks + 1)

    spans = [pl.ds(0, EARLY), pl.ds(EARLY, 2), pl.ds(EARLY + 2, 1)]
    for m in range(3):
        block = xg.at[c, spans[m]]
        net.go(block, block, g_in.at[m, c], far)
        net.go(block, block, g_in.at[m, c], twin)

    def chain_start(ref, sem):
        net.go(ref, ref, sem, right, z < n_space - 1)
        net.go(ref, ref, sem, left, z > 0)
        net.go(ref, ref, sem, across)

    def chain_step(d, ref_of, sem_of):
        for ok, zz, on, onward in (
            (z - d >= 0, jnp.maximum(z - d, 0), right, z < n_space - 1),
            (z + d < n_space, jnp.minimum(z + d, n_space - 1), left, z > 0),
        ):
            s = y * n_space + zz
            net.wait(ref_of(s), sem_of(s), left, ok)
            if d < n_space - 1:
                net.go(ref_of(s), ref_of(s), sem_of(s), on, ok & onward)
            net.go(ref_of(s), ref_of(s), sem_of(s), across, ok)

    def chain_end(zz, ref_of, sem_of, then=None):
        s = (1 - y) * n_space + zz
        net.wait(ref_of(s), sem_of(s), across)
        if then is not None:
            then(s)

    def row_start(ref, sem):
        for o in range(1, n_space):
            net.go(ref, ref, sem, (y, (z + o) % n_space, c))
        net.go(ref, ref, sem, across)

    def row_step(o, ref_of, sem_of, then=None):
        s = y * n_space + (z + o) % n_space
        net.wait(ref_of(s), sem_of(s), left)
        net.go(ref_of(s), ref_of(s), sem_of(s), across)
        if then is not None:
            then(s)

    rows = part // 2
    for row in range(n_dp):
        for zl in range(2):
            to = (row, 2 * core + zl, c)
            net.go(
                xg.at[c, pl.ds(4 * row, SHARE[row]), pl.ds(rows * zl, rows)],
                xb.at[chip, b, pl.ds(0, SHARE[row])], b_in.at[chip, b], to,
                jnp.logical_not((y == row) & (z == 2 * core + zl)),
            )

    def eight(s):
        return x8.at[c, s]

    def eight_sem(s):
        return e_in.at[s]

    net.go(w_hbm, w2.at[1], misc_in.at[0], twin)
    own_w.wait()
    own_g.wait()
    own_b.wait()

    def columns(t, first, count):
        return pl.ds(pl.multiple_of(t * width + first * part, 128), count * part)

    def forward_part(ch, ready, group, s, first):
        total = None if first else acc[4 * group + s]
        for t, tap in enumerate(TAPS):
            k = class_of(tap)
            if shift_of(tap[1], tap[2]) != s or (tap[0] == 0) != (group == 0) or k not in ready:
                continue
            term = jnp.dot(
                w2[0, :, columns(t, 2 * ch, 2)],
                xg[pl.ds(2 * ch, 2), k].reshape(2 * part, CELLS),
                preferred_element_type=F32,
            )
            total = term if total is None else total + term
        acc[4 * group + s] = total

    for m in range(3):
        net.wait(xg.at[twin[2], spans[m]], g_in.at[m, twin[2]], twin)
    relay = core == z // 2

    def relay_share(o):
        s = (b + o) % blocks
        for row in range(n_dp):
            block, ok = xb.at[chip, s, pl.ds(0, SHARE[row])], relay & (y == row)
            net.wait(block, b_in.at[chip, s], across, ok)
            net.go(block, block, b_in.at[chip, s], far, ok)
            net.go(block, block, b_in.at[chip, s], twin, ok)

    for s in range(4):
        for group in range(2):
            forward_part(chip, range(8), group, s, True)
    early, late = range(EARLY), range(EARLY, 8)
    other = 2 * (1 - chip) + 1 - core

    def far_arrived(m):
        net.wait(xg.at[cf, spans[m]], g_in.at[m, cf], far)
        net.go(xg.at[cf, spans[m]], xg.at[cf, spans[m]], g_in.at[m, cf], twin)

    def far_passed(m):
        net.wait(xg.at[other, spans[m]], g_in.at[m, other], twin)

    far_arrived(0)
    far_passed(0)
    for s in range(4):
        forward_part(1 - chip, early, 0, s, False)
    ahead = acc[0]
    for s in (1, 2, 3):
        ahead = ahead + forward_shift(acc[s], s)
    carry[0] = ahead
    net.go(carry.at[0], carry.at[1], misc_in.at[1], right, z < n_space - 1)
    row_start(x8.at[c, b], e_in.at[b])
    for s in range(4):
        forward_part(1 - chip, early, 1, s, False)
    far_arrived(1)
    far_arrived(2)
    far_passed(1)
    far_passed(2)
    for o in range(1, blocks):
        relay_share(o)

    for s in range(4):
        forward_part(1 - chip, late, 1, s, False)
    diagonal = lax.broadcasted_iota(jnp.int32, (part, part), 0) == lax.broadcasted_iota(jnp.int32, (part, part), 1)
    u = jnp.sum(jnp.where(diagonal, b_ref[...], 0.0), axis=1, keepdims=True) + acc[4]
    for s in (1, 2, 3):
        u = u + forward_shift(acc[4 + s], s)

    @pl.when(z == 0)
    def _():
        carry[1] = jnp.zeros_like(carry[1])

    net.wait(carry.at[1], misc_in.at[1], left, z > 0)
    u = u + carry[1]
    k0 = 0.7978845608028654
    th = jnp.tanh(k0 * (u + 0.044715 * (u * u * u)))
    slope = 0.5 * (1.0 + th) + 0.5 * u * (1.0 - th * th) * k0 * (1.0 + 3 * 0.044715 * u * u)
    dysh[0, b] = (g_ref[...].astype(F32) * slope).astype(BF)
    act_ref[...] = (0.5 * u * (1.0 + th)).astype(BF)

    def dy_of(s):
        return dysh.at[0, s]

    def dy_sem(s):
        return dy_in.at[s]

    row_start(dysh.at[0, b], dy_in.at[b])
    net.go(dysh.at[0, b], dyt.at[0, 0], dyt_in.at[0], twin)
    own_slots = []
    for hx in range(2):
        own_slots.append(
            pltpu.make_async_copy(
                xg.at[2 * hx + z // 2, pl.ds(4 * y, 4), pl.ds(pl.multiple_of(rows * (z % 2), rows), rows)],
                xb.at[hx, b],
                local_sem.at[1 + hx],
            )
        )
        own_slots[-1].start()

    def shift_slot(s):
        wide = dysh[0, s].astype(F32)
        for k in (1, 2, 3):
            dysh[k, s] = backward_shift(wide, k).astype(BF)

    for o in range(1, n_space):
        row_step(o, eight, eight_sem)
    shift_slot(b)
    for o in (1, 3, 2):
        row_step(o, dy_of, dy_sem)
    nxt = y * n_space + jnp.minimum(z + 1, n_space - 1)
    net.go(dysh.at[0, nxt], dyt.at[0, 1], dyt_in.at[1], twin, z < n_space - 1)
    for o in range(1, n_space):
        shift_slot(y * n_space + (z + o) % n_space)
    for zz in range(n_space):
        chain_end(zz, eight, eight_sem)

    for r in range(n_dp):
        mine = x8.at[c, pl.ds(n_space * r, n_space)]
        net.go(mine, mine, e_all.at[r, c], far)
        net.go(mine, mine, e_all.at[r, c], twin)
    for o in (0, 1, 3, 2):
        chain_end((z + o) % n_space, dy_of, dy_sem, shift_slot)

    for o in range(1, blocks):
        s = (b + o) % blocks
        for row in range(n_dp):
            net.wait(
                xb.at[chip, s, pl.ds(0, SHARE[row])], b_in.at[chip, s], twin, jnp.logical_not(relay) & (y == row)
            )
    for copy in own_slots:
        copy.wait()

    def share_half(row, i, side):
        _, (k1, k2, k3), k = share_taps(row)[i]
        total = None
        for v in range(n_dp):
            for zz in range(n_space - (k1 == 0)):
                s = v * n_space + zz
                term = lax.dot_general(
                    dysh[shift_of(k2, k3), s + (k1 == 0)], xb[side, s, k], NT, preferred_element_type=F32
                )
                total = term if total is None else total + term
        return total * scale

    def share_piece(row, i, side):
        first = 2 * (i % (PIECES // 2))
        low = share_half(row, first, side)
        high = share_half(row, first + 1, side) if first + 1 < len(share_taps(row)) else jnp.zeros_like(low)
        dwb_ref[b, i] = jnp.concatenate([low, high], axis=1).astype(BF)

    def dw_of(m):
        lo, hi = CHUNKS[m]
        return lambda s: dwb_ref.at[s, pl.ds(lo, hi - lo)]

    def dw_sem(m):
        return lambda s: dw_in.at[m, s]

    def share_chunk(m):
        lo, hi = CHUNKS[m]
        for row in range(n_dp):
            @pl.when(y == row)
            def _():
                for i in range(lo, hi):
                    share_piece(row, i, chip if i < PIECES // 2 else 1 - chip)
        chain_start(dw_of(m)(b), dw_sem(m)(b))

    for m in (0, 1):
        share_chunk(m)
    for o in range(1, blocks):
        s = (b + o) % blocks
        for row in range(n_dp):
            other_half, ok = xb.at[1 - chip, s, pl.ds(0, SHARE[row])], relay & (y == row)
            net.wait(other_half, b_in.at[1 - chip, s], far, ok)
            net.go(other_half, other_half, b_in.at[1 - chip, s], twin, ok)
    for o in range(1, blocks):
        s = (b + o) % blocks
        for row in range(n_dp):
            net.wait(
                xb.at[1 - chip, s, pl.ds(0, SHARE[row])], b_in.at[1 - chip, s], twin,
                jnp.logical_not(relay) & (y == row),
            )
    for m in (2, 3):
        share_chunk(m)

    @pl.when(z == n_space - 1)
    def _():
        dyt[0, 1] = jnp.zeros_like(dyt[0, 1])

    net.wait(dyt.at[0, 0], dyt_in.at[0], twin)
    net.wait(dyt.at[0, 1], dyt_in.at[1], twin, z < n_space - 1)
    for i in range(2):
        wide = dyt[0, i].astype(F32)
        for k in (1, 2, 3):
            dyt[k, i] = backward_shift(wide, k).astype(BF)
    net.wait(w2.at[1], misc_in.at[0], twin)
    edge = jnp.where(z < n_space - 1, 1.0, 0.0).astype(BF)

    def input_grad(j, p, ph):
        total = None
        for t, (k1, k2, k3) in enumerate(TAPS):
            if phase_of(k2, k3) != ph or (k1 != 1) != (p == 1):
                continue
            s = shift_of(k2, k3)
            here = dysh[s, nxt] * edge if k1 == 0 else dysh[s, b]
            for i, view in enumerate((here, dyt[s, int(k1 == 0)])):
                term = lax.dot_general(
                    w2[i, :, columns(t, j, 1)], view, TN, preferred_element_type=F32
                )
                total = term if total is None else total + term
        return total

    for p in range(2):
        for ph in range(4):
            gx_far[p, ph] = input_grad(cf, p, ph).astype(BF)
        net.go(gx_far.at[p], gx_in.at[p], gx_sem.at[p], far)

    def pass_on(d, *chunks):
        for m in chunks:
            chain_step(d, dw_of(m), dw_sem(m))

    pass_on(1, 0, 1)
    for ph in range(4):
        gx_own[0, ph] = input_grad(c, 0, ph)
    pass_on(1, 2, 3)
    for ph in range(4):
        gx_own[1, ph] = input_grad(c, 1, ph)
    pass_on(2, 0, 1)

    for r in range(n_dp):
        theirs = x8.at[cf, pl.ds(n_space * r, n_space)]
        net.wait(theirs, e_all.at[r, cf], far)
        net.go(theirs, theirs, e_all.at[r, cf], twin)
    pass_on(2, 2, 3)
    for r in range(n_dp):
        for j in (twin[2], other):
            net.wait(x8.at[j, pl.ds(n_space * r, n_space)], e_all.at[r, j], twin)
    for k in range(2):
        for v in range(n_dp):
            for zz in range(n_space - (k == 0)):
                s = v * n_space + zz
                term = lax.dot_general(
                    dysh[:, s + (k == 0)].reshape(4 * part, CELLS),
                    x8[:, s].reshape(n_chan * part, CELLS),
                    NT,
                    preferred_element_type=F32,
                ) * scale
                if s == 0:
                    d8_ref[k] = term
                else:
                    d8_ref[k] += term
        pass_on(3, *((0, 1) if k == 0 else (2, 3)))
    ones = jnp.ones((8, CELLS), BF)
    total = None
    for s in range(blocks):
        term = lax.dot_general(ones, dysh[0, s], NT, preferred_element_type=F32)
        total = term if total is None else total + term
    db_ref[...] = total * scale

    for p in range(2):
        net.wait(gx_in.at[p], gx_sem.at[p], far)
    for p in range(2):
        cells = [(gx_own[p, ph] + gx_in[p, ph].astype(F32)).astype(BF) for ph in range(4)]
        for h in range(2):
            strip = jnp.concatenate([cell[:, h * half : (h + 1) * half] for cell in cells], axis=1)
            gx_ref[p, :, 2 * CELLS * h : 2 * CELLS * (h + 1)] = lax.dot_general(
                strip, parity_block(), NT, preferred_element_type=F32
            ).astype(BF)
    for m in range(len(CHUNKS)):
        for zz in range(n_space):
            chain_end(zz, dw_of(m), dw_sem(m))
    net.drain()


def finish_kernel(n_space, part, dwb_ref, d8_ref, gx_ref, act_ref, db_ref, act_out, gx_out, dw_out, db_out, wide, sem):
    chip = lax.axis_index("chan") // 2
    copies = [
        pltpu.make_async_copy(gx_ref, gx_out, sem.at[len(TAPS)]),
        pltpu.make_async_copy(act_ref, act_out, sem.at[len(TAPS) + 1]),
    ]
    for copy in copies:
        copy.start()
    db_out[...] = db_ref[0:1]
    width = 4 * part
    where = {}
    for row in range(2):
        for i, (t, _, _) in enumerate(share_taps(row)):
            where[t] = (row, i)
    low = lax.broadcasted_iota(jnp.int32, (part, part), 1) < part // 2
    for t in sorted(range(len(TAPS)), key=lambda t: t in where):
        k1, k2, k3 = TAPS[t]
        first = t * width
        if t in where:
            row, i = where[t]
            for j in range(4):
                q = i // 2 + PIECES // 2 * jnp.where(chip == j // 2, 0, 1)
                even = dwb_ref[row * n_space + 2 * (j % 2), q].astype(F32)
                odd = dwb_ref[row * n_space + 2 * (j % 2) + 1, q].astype(F32)
                if i % 2:
                    even = pltpu.roll(even, part // 2, 1)
                else:
                    odd = pltpu.roll(odd, part // 2, 1)
                wide[:, first + j * part : first + (j + 1) * part] = jnp.where(low, even, odd)
        else:
            s = shift_of(k2, k3)
            wide[:, first : first + width] = d8_ref[int(k1 == 2), s * part : (s + 1) * part]
        span = pl.ds(first, width)
        copies.append(pltpu.make_async_copy(wide.at[:, span], dw_out.at[:, span], sem.at[t]))
        copies[-1].start()
    for copy in copies:
        copy.wait()


def per_device_shared(volumes, kernel, bias, act_grad):
    batch, planes, part, cells = volumes.shape
    filters = kernel.shape[0]
    width = kernel.shape[1] // 27
    sizes = tuple(lax.axis_size(a) for a in ("dp", "space", "chan"))
    n_dp, n_space, n_chan = sizes
    blocks = n_dp * n_space
    dma = pltpu.SemaphoreType.DMA
    flops = 2 * 27 * width * filters * CELLS
    ANY = pl.BlockSpec(memory_space=pl.ANY)
    act, gx, dwb, d8, db = pl.pallas_call(
        functools.partial(layer_kernel, sizes, width, 1.0 / (batch * n_dp)),
        out_shape=(
            shape(filters, CELLS),
            shape(planes, part, cells),
            shape(blocks, PIECES, filters, part),
            shape(2, 4 * filters, width, dtype=F32),
            shape(8, filters, dtype=F32),
        ),
        in_specs=[ANY] * 4,
        out_specs=[VM] * 5,
        scratch_shapes=(
            pltpu.VMEM((planes, part, cells), BF),
            pltpu.VMEM((filters, CELLS), BF),
            pltpu.VMEM((1, filters), F32),
            pltpu.VMEM((2, filters, 27 * width), BF),
            pltpu.VMEM((n_chan, 8, part, CELLS), BF),
            pltpu.VMEM((2, blocks, 4, part // 2, CELLS), BF),
            pltpu.VMEM((n_chan, blocks, part, CELLS), BF),
            pltpu.VMEM((8, filters, CELLS), F32),
            pltpu.VMEM((2, filters, CELLS), F32),
            pltpu.VMEM((4, blocks, filters, CELLS), BF),
            pltpu.VMEM((4, 2, filters, CELLS), BF),
            pltpu.VMEM((2, 4, part, CELLS), BF),
            pltpu.VMEM((2, 4, part, CELLS), BF),
            pltpu.VMEM((2, 4, part, CELLS), F32),
            dma((SENDS,)),
            dma((6,)),
            dma((3, n_chan)),
            dma((2, blocks)),
            dma((blocks,)),
            dma((n_dp, n_chan)),
            dma((blocks,)),
            dma((2,)),
            dma((len(CHUNKS), blocks)),
            dma((2,)),
            dma((2,)),
        ),
        compiler_params=pltpu.CompilerParams(
            vmem_limit_bytes=46 << 20, collective_id=0, has_side_effects=True
        ),
        cost_estimate=pl.CostEstimate(flops=5 * flops, bytes_accessed=12 << 20, transcendentals=0),
    )(
        *(
            pltpu.with_memory_space_constraint(array, pltpu.HBM)
            for array in (
                volumes.reshape(planes, part, cells),
                kernel,
                bias.reshape(1, filters),
                act_grad.reshape(filters, CELLS),
            )
        )
    )
    act, gx, dw, db = pl.pallas_call(
        functools.partial(finish_kernel, n_space, part),
        out_shape=(
            shape(filters, CELLS),
            shape(planes, part, cells),
            shape(filters, 27 * width, dtype=F32),
            shape(1, filters, dtype=F32),
        ),
        in_specs=[VM] * 5,
        out_specs=[ANY, ANY, ANY, VM],
        scratch_shapes=(pltpu.VMEM((filters, 27 * width), F32), dma((len(TAPS) + 2,))),
        compiler_params=pltpu.CompilerParams(vmem_limit_bytes=40 << 20),
        cost_estimate=pl.CostEstimate(flops=0, bytes_accessed=12 << 20, transcendentals=0),
    )(dwb, d8, gx, act, db)
    return act.reshape(act_grad.shape), gx.reshape(volumes.shape), dw, db.reshape(filters)


def solution(mesh):
    shared = (mesh.shape["dp"], mesh.shape["space"], mesh.shape["chan"]) == (2, 4, 4)
    in_specs = (
        P("dp", "space", "chan", None),
        P("chan", None),
        P("chan"),
        P("dp", "space", "chan", None),
    )
    out_specs = (
        P("dp", "space", "chan", None),
        P("dp", "space", "chan", None),
        P("chan", None),
        P("chan"),
    )
    return jax.shard_map(
        per_device_shared if shared else per_device,
        mesh=mesh, in_specs=in_specs, out_specs=out_specs, check_vma=False,
    )
```

```python
import functools

import jax
import jax.numpy as jnp
from jax import lax
from jax.experimental import pallas as pl
from jax.experimental.pallas import tpu as pltpu
from jax.sharding import PartitionSpec as P

GRID = 32
HALF = GRID // 2
CELLS = HALF * HALF
BF = jnp.bfloat16
F32 = jnp.float32
VM = pl.BlockSpec(memory_space=pltpu.VMEM)
TAPS = [(k1, k2, k3) for k1 in range(3) for k2 in range(3) for k3 in range(3)]


def phase_of(k2, k3):
    return 2 * (k2 != 1) + (k3 != 1)


def shift_of(k2, k3):
    return 2 * (k2 == 0) + (k3 == 0)


def parity_matrix():
    full = GRID * GRID
    dst = lax.broadcasted_iota(jnp.int32, (1, full), 1)
    phase, cell = dst // CELLS, dst % CELLS
    y = 2 * (cell // HALF) + phase // 2
    z = 2 * (cell % HALF) + phase % 2
    src = y * GRID + z
    rows = lax.broadcasted_iota(jnp.int32, (full, full), 0)
    return jnp.where(rows == src, 1.0, 0.0).astype(BF)


def lanes():
    return lax.broadcasted_iota(jnp.int32, (1, CELLS), 1)


def forward_shift(x, s):
    if s & 2:
        x = jnp.where(lanes() >= HALF, pltpu.roll(x, HALF, 1), 0.0)
    if s & 1:
        x = jnp.where(lanes() % HALF != 0, pltpu.roll(x, 1, 1), 0.0)
    return x


def backward_shift(x, s):
    if s & 2:
        x = jnp.where(lanes() < CELLS - HALF, pltpu.roll(x, CELLS - HALF, 1), 0.0)
    if s & 1:
        x = jnp.where(lanes() % HALF != HALF - 1, pltpu.roll(x, CELLS - 1, 1), 0.0)
    return x


def split_kernel(v_ref, p_ref, o_ref):
    o_ref[...] = jnp.dot(v_ref[...], p_ref[...], preferred_element_type=F32).astype(BF)


def merge_kernel(v_ref, p_ref, o_ref):
    total = v_ref[0].astype(F32)
    for j in range(1, v_ref.shape[0]):
        total = total + v_ref[j].astype(F32)
    o_ref[...] = lax.dot_general(
        total.astype(BF).reshape(o_ref.shape), p_ref[...], (((1,), (1,)), ((), ())), preferred_element_type=F32
    ).astype(BF)


def send(src, dst, send_sem, recv_sem, device):
    return pltpu.make_async_remote_copy(
        src, dst, send_sem, recv_sem, device_id=device, device_id_type=pl.DeviceIdType.MESH
    )


def place():
    return lax.axis_index("dp"), lax.axis_index("space"), lax.axis_index("chan")


def greet(sizes):
    n_dp, n_space, n_chan = sizes
    y, z, c = place()
    barrier = pltpu.get_barrier_semaphore()
    g = y * n_space + z
    for o in range(1, n_chan):
        pl.semaphore_signal(
            barrier, 1, device_id=(y, z, (c + o) % n_chan), device_id_type=pl.DeviceIdType.MESH
        )
    for o in range(1, n_dp * n_space):
        h = (g + o) % (n_dp * n_space)
        pl.semaphore_signal(
            barrier, 1, device_id=(h // n_space, h % n_space, c), device_id_type=pl.DeviceIdType.MESH
        )
    pl.semaphore_wait(barrier, n_chan + n_dp * n_space - 2)


def gather_inputs(sizes, own_ref, x_ref, out_sem, in_sem, local_sem):
    n_dp, n_space, n_chan = sizes
    chips = n_chan // 2
    y, z, c = place()
    chip, core = c // 2, c % 2
    twin = (y, z, 2 * chip + 1 - core)
    greet(sizes)

    def planes(k):
        return pl.ds(1, 2) if k else pl.ds(0, 1)

    def block(k, j):
        return x_ref.at[planes(k), j]

    def to_chip(k, o, src):
        return send(
            src, block(k, c), out_sem.at[k, 0, o], in_sem.at[k, c],
            (y, z, 2 * ((chip + o) % chips) + core),
        )

    def to_twin(k, o, src):
        j = 2 * ((chip - o + chips) % chips) + core
        return send(src, block(k, j), out_sem.at[k, 1, o], in_sem.at[k, j], twin)

    def arrived(k, j):
        send(block(k, j), block(k, j), out_sem.at[k, 1, 0], in_sem.at[k, j], twin).wait_recv()

    rim = send(own_ref.at[pl.ds(1, 1)], block(0, c), out_sem.at[0, 2, 0], in_sem.at[0, c], (y, jnp.minimum(z + 1, n_space - 1), c))
    sends = [to_chip(1, o, own_ref) for o in range(1, chips)] + [to_twin(1, 0, own_ref)]

    @pl.when(z < n_space - 1)
    def _():
        rim.start()

    for copy in sends:
        copy.start()
    keep = pltpu.make_async_copy(own_ref, block(1, c), local_sem)
    keep.start()

    rim_out = [to_chip(0, o, block(0, c)) for o in range(1, chips)] + [to_twin(0, 0, block(0, c))]

    @pl.when(z > 0)
    def _():
        arrived(0, c)
        for copy in rim_out:
            copy.start()

    @pl.when(z == 0)
    def _():
        x_ref[0] = jnp.zeros_like(x_ref[0])

    for o in range(1, chips):
        j = 2 * ((chip - o + chips) % chips) + core
        arrived(1, j)
        passed = to_twin(1, o, block(1, j))
        passed.start()
        sends.append(passed)

    @pl.when(z > 0)
    def _():
        for o in range(1, chips):
            j = 2 * ((chip - o + chips) % chips) + core
            arrived(0, j)
            passed = to_twin(0, o, block(0, j))
            passed.start()
            rim_out.append(passed)
        for o in range(chips):
            arrived(0, 2 * ((chip - o + chips) % chips) + 1 - core)
        for copy in rim_out:
            copy.wait_send()

    for o in range(chips):
        arrived(1, 2 * ((chip - o + chips) % chips) + 1 - core)
    for copy in sends:
        copy.wait_send()

    @pl.when(z < n_space - 1)
    def _():
        rim.wait_send()

    keep.wait()


def forward_kernel(
    sizes, width, own_ref, w_ref, b_ref, g_ref, x_ref, act_ref, dy_ref, db_ref, out_sem, in_sem, local_sem
):
    gather_inputs(sizes, own_ref, x_ref, out_sem, in_sem, local_sem)
    sums = [None] * 4
    for t, (k1, k2, k3) in enumerate(TAPS):
        ph, s = phase_of(k2, k3), shift_of(k2, k3)
        part = jnp.dot(
            w_ref[:, t * width : (t + 1) * width],
            x_ref[k1, :, :, ph * CELLS : (ph + 1) * CELLS].reshape(width, CELLS),
            preferred_element_type=F32,
        )
        sums[s] = part if sums[s] is None else sums[s] + part
    u = b_ref[...] + sums[0]
    for s in (1, 2, 3):
        u = u + forward_shift(sums[s], s)
    c = 0.7978845608028654
    th = jnp.tanh(c * (u + 0.044715 * (u * u * u)))
    act_ref[...] = (0.5 * u * (1.0 + th)).astype(BF)
    slope = 0.5 * (1.0 + th) + 0.5 * u * (1.0 - th * th) * c * (1.0 + 3 * 0.044715 * u * u)
    dy = (g_ref[...].astype(F32) * slope).astype(BF)
    dy_ref[...] = dy
    db_ref[...] = lax.dot_general(
        jnp.ones((8, CELLS), BF), dy, (((1,), (1,)), ((), ())), preferred_element_type=F32
    )


def shifted(dy):
    wide = dy.astype(F32)
    return [dy] + [backward_shift(wide, s).astype(BF) for s in (1, 2, 3)]


def grads_kernel(sizes, width, x_ref, w_ref, dy_ref, dw_ref, gx_ref, next_ref, out_sem, in_sem):
    n_space = sizes[1]
    y, z, c = place()
    greet(sizes)
    back = send(dy_ref, next_ref, out_sem, in_sem, (y, jnp.maximum(z - 1, 0), c))

    @pl.when(z > 0)
    def _():
        back.start()

    own = shifted(dy_ref[...])
    for t, (k1, k2, k3) in enumerate(TAPS):
        ph, s = phase_of(k2, k3), shift_of(k2, k3)
        part = lax.dot_general(
            own[s],
            x_ref[k1, :, :, ph * CELLS : (ph + 1) * CELLS].reshape(width, CELLS),
            (((1,), (1,)), ((), ())),
            preferred_element_type=F32,
        )
        dw_ref[:, t * width : (t + 1) * width] = part.astype(BF)

    @pl.when(z < n_space - 1)
    def _():
        back.wait_recv()

    @pl.when(z == n_space - 1)
    def _():
        next_ref[...] = jnp.zeros_like(next_ref)

    following = shifted(next_ref[...])
    for plane in range(2):
        for ph in range(4):
            total = None
            for t, (k1, k2, k3) in enumerate(TAPS):
                if phase_of(k2, k3) != ph or (k1 == 1) != (plane == 0):
                    continue
                views = following if k1 == 0 else own
                part = lax.dot_general(
                    w_ref[:, t * width : (t + 1) * width],
                    views[shift_of(k2, k3)],
                    (((0,), (0,)), ((), ())),
                    preferred_element_type=F32,
                )
                total = part if total is None else total + part
            gx_ref[:, plane, :, ph * CELLS : (ph + 1) * CELLS] = total.astype(BF).reshape(
                gx_ref.shape[0], gx_ref.shape[2], CELLS
            )

    @pl.when(z > 0)
    def _():
        back.wait_send()


def share_kernel(
    sizes, dw_ref, gx_ref, db_ref, all_ref, parts_ref, dbs_ref, y_ref, r_ref, l_ref, s_ref,
    out_sem, in_sem, gx_out, gx_in, db_out, db_in, local_sem, y_out, y_in, z_out, r_in, l_in
):
    n_dp, n_space, n_chan = sizes
    group = n_dp * n_space
    y, z, c = place()
    g = y * n_space + z
    greet(sizes)
    right = (y, jnp.minimum(z + 1, n_space - 1), c)
    left = (y, jnp.maximum(z - 1, 0), c)
    across = (1 - y, z, c)

    def hop(way, device, j, src=None):
        slot = all_ref.at[y * n_space + j]
        return send(slot if src is None else src, slot, out_sem.at[way, j], in_sem.at[y * n_space + j], device)

    def arrived(h):
        send(all_ref.at[h], all_ref.at[h], out_sem.at[2, 0], in_sem.at[h], across).wait_recv()

    locals_ = [
        pltpu.make_async_copy(gx_ref.at[c], parts_ref.at[c], local_sem.at[1]),
        pltpu.make_async_copy(db_ref, dbs_ref.at[g], local_sem.at[2]),
    ]

    def over(j):
        return send(dw_ref.at[(1 - y) * n_space + j], y_ref.at[j], y_out.at[j], y_in.at[j], across)

    def rightward(j):
        return send(s_ref.at[j], r_ref.at[j], z_out.at[j], r_in.at[j], right)

    def leftward(j):
        return send(s_ref.at[j], l_ref.at[j], z_out.at[j], l_in.at[j], left)

    def both(j):
        over(j).wait_recv()
        return dw_ref[y * n_space + j].astype(F32) + y_ref[j].astype(F32)

    for d in range(n_space - 1, 0, -1):
        @pl.when(z + d < n_space)
        def _():
            over(jnp.minimum(z + d, n_space - 1)).start()

        @pl.when(z - d >= 0)
        def _():
            over(jnp.maximum(z - d, 0)).start()

    over(z).start()
    extra = []
    for o in range(1, n_chan):
        to = (c + o) % n_chan
        extra.append(
            send(gx_ref.at[to], parts_ref.at[c], gx_out.at[o], gx_in.at[o], (y, z, to))
        )
    for o in range(1, group):
        to = (g + o) % group
        extra.append(
            send(db_ref, dbs_ref.at[g], db_out.at[o], db_in.at[o], (to // n_space, to % n_space, c))
        )
    for copy in extra:
        copy.start()
    for copy in locals_:
        copy.start()

    for d in range(n_space - 1, 0, -1):
        @pl.when(z + d < n_space)
        def _():
            j = jnp.minimum(z + d, n_space - 1)
            mine = both(j)

            @pl.when(z == 0)
            def _():
                s_ref[j] = mine.astype(BF)

            @pl.when(z > 0)
            def _():
                rightward(j).wait_recv()
                s_ref[j] = (mine + r_ref[j].astype(F32)).astype(BF)

            rightward(j).start()

        @pl.when(z - d >= 0)
        def _():
            j = jnp.maximum(z - d, 0)
            mine = both(j)

            @pl.when(z == n_space - 1)
            def _():
                s_ref[j] = mine.astype(BF)

            @pl.when(z < n_space - 1)
            def _():
                leftward(j).wait_recv()
                s_ref[j] = (mine + l_ref[j].astype(F32)).astype(BF)

            leftward(j).start()

    @pl.when(z == 0)
    def _():
        r_ref[z] = jnp.zeros_like(r_ref[z])

    @pl.when(z == n_space - 1)
    def _():
        l_ref[z] = jnp.zeros_like(l_ref[z])

    @pl.when(z > 0)
    def _():
        rightward(z).wait_recv()

    @pl.when(z < n_space - 1)
    def _():
        leftward(z).wait_recv()

    all_ref[g] = (both(z) + r_ref[z].astype(F32) + l_ref[z].astype(F32)).astype(BF)

    @pl.when(z < n_space - 1)
    def _():
        hop(0, right, z).start()

    @pl.when(z > 0)
    def _():
        hop(1, left, z).start()

    hop(2, across, z).start()

    for d in range(1, n_space):
        @pl.when(z - d >= 0)
        def _():
            j = jnp.maximum(z - d, 0)
            arrived(y * n_space + j)

            @pl.when(z < n_space - 1)
            def _():
                hop(0, right, j).start()

            hop(2, across, j).start()

        @pl.when(z + d < n_space)
        def _():
            j = jnp.minimum(z + d, n_space - 1)
            arrived(y * n_space + j)

            @pl.when(z > 0)
            def _():
                hop(1, left, j).start()

            hop(2, across, j).start()

    for o in range(1, n_chan):
        frm = (c - o + n_chan) % n_chan
        send(parts_ref.at[frm], parts_ref.at[frm], gx_out.at[o], gx_in.at[o], (y, z, frm)).wait_recv()
    for o in range(1, group):
        frm = (g - o + group) % group
        send(dbs_ref.at[frm], dbs_ref.at[frm], db_out.at[o], db_in.at[o], (frm // n_space, frm % n_space, c)).wait_recv()
    for j in range(n_space):
        arrived((1 - y) * n_space + j)
        hop(2, across, j).wait_send()

        @pl.when((j <= z) & (z < n_space - 1))
        def _():
            hop(0, right, j).wait_send()

        @pl.when((j >= z) & (z > 0))
        def _():
            hop(1, left, j).wait_send()

        over(j).wait_send()

        @pl.when(j > z)
        def _():
            rightward(j).wait_send()

        @pl.when(j < z)
        def _():
            leftward(j).wait_send()

    for copy in extra:
        copy.wait_send()
    for copy in locals_:
        copy.wait()


def call(kernel, out_shape, n_in, flops, moved, scratch=(), collective_id=None):
    many = isinstance(out_shape, (tuple, list))
    return pl.pallas_call(
        kernel,
        out_shape=out_shape,
        in_specs=[VM] * n_in,
        out_specs=[VM] * len(out_shape) if many else VM,
        scratch_shapes=scratch,
        compiler_params=pltpu.CompilerParams(
            vmem_limit_bytes=48 << 20,
            collective_id=collective_id,
            has_side_effects=collective_id is not None,
        ),
        cost_estimate=pl.CostEstimate(flops=flops, bytes_accessed=moved, transcendentals=0),
    )


def shape(*dims, dtype=BF):
    return jax.ShapeDtypeStruct(dims, dtype)


def per_device(volumes, kernel, bias, act_grad):
    batch, planes, part, cells = volumes.shape
    filters = kernel.shape[0]
    width = kernel.shape[1] // 27
    parity = parity_matrix()
    own = call(split_kernel, shape(planes * part, cells), 2, 2 * planes * part * cells**2, 1 << 20)(
        volumes.reshape(planes * part, cells), parity
    ).reshape(planes, part, cells)
    sizes = tuple(lax.axis_size(a) for a in ("dp", "space", "chan"))
    group, n_chan = sizes[0] * sizes[1], sizes[2]
    dma = pltpu.SemaphoreType.DMA
    flops = 2 * 27 * width * filters * CELLS
    x_all, act, dy, db = call(
        functools.partial(forward_kernel, sizes, width),
        (
            shape(3, n_chan, part, cells),
            shape(filters, CELLS),
            shape(filters, CELLS),
            shape(8, filters, dtype=F32),
        ),
        4,
        flops,
        10 << 20,
        scratch=(dma((2, 3, n_chan // 2)), dma((2, n_chan)), dma),
        collective_id=0,
    )(own, kernel, bias.reshape(filters, 1), act_grad.reshape(filters, CELLS))
    dw, gx = call(
        functools.partial(grads_kernel, sizes, width),
        (shape(filters, 27 * width), shape(n_chan, planes, part, cells)),
        3,
        3 * flops,
        12 << 20,
        scratch=(pltpu.VMEM((filters, CELLS), BF), dma, dma),
        collective_id=2,
    )(x_all, kernel, dy)
    count = batch * sizes[0]
    rows = filters // group
    slots = pltpu.VMEM((sizes[1], rows, 27 * width), BF)
    dw_all, parts, dbs = call(
        functools.partial(share_kernel, sizes),
        (
            shape(group, rows, 27 * width),
            shape(n_chan, planes, part, cells),
            shape(group, 8, filters, dtype=F32),
        ),
        3,
        0,
        12 << 20,
        scratch=(
            slots,
            slots,
            slots,
            slots,
            dma((3, sizes[1])),
            dma((group,)),
            dma((n_chan,)),
            dma((n_chan,)),
            dma((group,)),
            dma((group,)),
            dma((3,)),
            dma((sizes[1],)),
            dma((sizes[1],)),
            dma((sizes[1],)),
            dma((sizes[1],)),
            dma((sizes[1],)),
        ),
        collective_id=1,
    )(dw.reshape(group, rows, 27 * width), gx, db)
    grad_w = dw_all.reshape(filters, 27 * width).astype(F32) / count
    grad_b = jnp.sum(dbs[:, 0], axis=0) / count
    grad_x = call(merge_kernel, shape(planes * part, cells), 2, 2 * planes * part * cells**2, 1 << 20)(
        parts, parity
    )
    return (
        act.reshape(act_grad.shape),
        grad_x.reshape(volumes.shape),
        grad_w,
        grad_b,
    )


ORDER = [(0, 1), (1, 1), (1, 2), (1, 3), (1, 0), (0, 0), (0, 2), (0, 3)]
EIGHT = ORDER.index((1, 3))
EARLY = 5
SHARE = (3, 4)
PIECES = 10
CHUNKS = [(0, 2), (2, 5), (5, 7), (7, 10)]
NT = (((1,), (1,)), ((), ()))
TN = (((0,), (0,)), ((), ()))


def class_of(tap):
    return ORDER.index((int(tap[0] != 1), phase_of(tap[1], tap[2])))


def share_taps(row):
    return [
        (t, tap, class_of(tap) - 4 * row)
        for k in range(4 * row, 4 * row + 4)
        for t, tap in enumerate(TAPS)
        if class_of(tap) == k and k != EIGHT
    ]


def parity_block():
    side = 2 * CELLS
    row = lax.broadcasted_iota(jnp.int32, (side, side), 0)
    col = lax.broadcasted_iota(jnp.int32, (side, side), 1)
    y, z = row // GRID, row % GRID
    dst = (2 * (y % 2) + z % 2) * (CELLS // 2) + (y // 2) * HALF + z // 2
    return jnp.where(dst == col, 1.0, 0.0).astype(BF)


class Net:
    def __init__(self, out_sem):
        self.out_sem, self.count, self.started = out_sem, 0, []

    def go(self, src, dst, in_sem, device, cond=None):
        copy = send(src, dst, self.out_sem.at[self.count], in_sem, device)
        self.count += 1
        self.started.append((copy, cond))
        if cond is None:
            copy.start()
        else:
            pl.when(cond)(copy.start)

    def wait(self, dst, in_sem, device, cond=None):
        copy = send(dst, dst, self.out_sem.at[0], in_sem, device)
        if cond is None:
            copy.wait_recv()
        else:
            pl.when(cond)(copy.wait_recv)

    def drain(self):
        for copy, cond in self.started:
            if cond is None:
                copy.wait_send()
            else:
                pl.when(cond)(copy.wait_send)


SENDS = 160


def layer_kernel(
    sizes, width, scale, v_hbm, w_hbm, b_hbm, g_hbm,
    act_ref, gx_ref, dwb_ref, d8_ref, db_ref,
    v_ref, g_ref, b_ref, w2, xg, xb, x8, acc, carry, dysh, dyt, gx_far, gx_in, gx_own,
    out_sem, local_sem, g_in, b_in, e_in, e_all, dy_in, dyt_in, dw_in, gx_sem, misc_in,
):
    n_dp, n_space, n_chan = sizes
    blocks = n_dp * n_space
    y, z, c = place()
    chip, core = c // 2, c % 2
    b = y * n_space + z
    twin = (y, z, 2 * chip + 1 - core)
    far = (y, z, 2 * (1 - chip) + core)
    cf = 2 * (1 - chip) + core
    right = (y, jnp.minimum(z + 1, n_space - 1), c)
    left = (y, jnp.maximum(z - 1, 0), c)
    across = (1 - y, z, c)
    net = Net(out_sem)

    own_v = pltpu.make_async_copy(v_hbm, v_ref, local_sem.at[3])
    own_v.start()
    own_g = pltpu.make_async_copy(g_hbm, g_ref, local_sem.at[4])
    own_g.start()
    own_b = pltpu.make_async_copy(b_hbm, b_ref, local_sem.at[5])
    own_b.start()
    barrier = pltpu.get_barrier_semaphore()
    for device in (twin, far):
        pl.semaphore_signal(barrier, 1, device_id=device, device_id_type=pl.DeviceIdType.MESH)
    for o in range(1, blocks):
        h = (b + o) % blocks
        pl.semaphore_signal(
            barrier, 1, device_id=(h // n_space, h % n_space, c), device_id_type=pl.DeviceIdType.MESH
        )
    own_w = pltpu.make_async_copy(w_hbm, w2.at[0], local_sem.at[0])
    own_w.start()

    part = v_ref.shape[1]
    half = CELLS // 2
    parity = parity_block()
    own_v.wait()
    for h in range(2):
        r = jnp.dot(
            v_ref[:, :, 2 * CELLS * h : 2 * CELLS * (h + 1)].reshape(2 * part, 2 * CELLS), parity,
            preferred_element_type=F32,
        ).astype(BF)
        for k, (p, ph) in enumerate(ORDER):
            tile = r[p * part : (p + 1) * part, ph * half : (ph + 1) * half]
            xg[c, k, :, h * half : (h + 1) * half] = tile
            if k == EIGHT:
                x8[c, b, :, h * half : (h + 1) * half] = tile

    pl.semaphore_wait(barrier, blocks + 1)

    spans = [pl.ds(0, EARLY), pl.ds(EARLY, 2), pl.ds(EARLY + 2, 1)]
    for m in range(3):
        block = xg.at[c, spans[m]]
        net.go(block, block, g_in.at[m, c], far)
        net.go(block, block, g_in.at[m, c], twin)

    def chain_start(ref, sem):
        net.go(ref, ref, sem, right, z < n_space - 1)
        net.go(ref, ref, sem, left, z > 0)
        net.go(ref, ref, sem, across)

    def chain_step(d, ref_of, sem_of):
        for ok, zz, on, onward in (
            (z - d >= 0, jnp.maximum(z - d, 0), right, z < n_space - 1),
            (z + d < n_space, jnp.minimum(z + d, n_space - 1), left, z > 0),
        ):
            s = y * n_space + zz
            net.wait(ref_of(s), sem_of(s), left, ok)
            if d < n_space - 1:
                net.go(ref_of(s), ref_of(s), sem_of(s), on, ok & onward)
            net.go(ref_of(s), ref_of(s), sem_of(s), across, ok)

    def chain_end(zz, ref_of, sem_of, then=None):
        s = (1 - y) * n_space + zz
        net.wait(ref_of(s), sem_of(s), across)
        if then is not None:
            then(s)

    def row_start(ref, sem):
        for o in range(1, n_space):
            net.go(ref, ref, sem, (y, (z + o) % n_space, c))
        net.go(ref, ref, sem, across)

    side = z // 2
    nearest = (z + 1 - 2 * side, 2 - 2 * z + 5 * side, 3 - 3 * side)

    def row_step(k, ref_of, sem_of, then=None):
        s = y * n_space + nearest[k]
        net.wait(ref_of(s), sem_of(s), left)
        net.go(ref_of(s), ref_of(s), sem_of(s), across)
        if then is not None:
            then(s)

    rows = part // 2
    for row in range(n_dp):
        for zl in range(2):
            to = (row, 2 * core + zl, c)
            net.go(
                xg.at[c, pl.ds(4 * row, SHARE[row]), pl.ds(rows * zl, rows)],
                xb.at[chip, b, pl.ds(0, SHARE[row])], b_in.at[chip, b], to,
                jnp.logical_not((y == row) & (z == 2 * core + zl)),
            )

    def eight(s):
        return x8.at[c, s]

    def eight_sem(s):
        return e_in.at[s]

    net.go(w_hbm, w2.at[1], misc_in.at[0], twin)
    own_w.wait()
    own_g.wait()
    own_b.wait()

    def columns(t, first, count):
        return pl.ds(pl.multiple_of(t * width + first * part, 128), count * part)

    def forward_part(ch, ready, group, s, first):
        total = None if first else acc[4 * group + s]
        for t, tap in enumerate(TAPS):
            k = class_of(tap)
            if shift_of(tap[1], tap[2]) != s or (tap[0] == 0) != (group == 0) or k not in ready:
                continue
            term = jnp.dot(
                w2[0, :, columns(t, 2 * ch, 2)],
                xg[pl.ds(2 * ch, 2), k].reshape(2 * part, CELLS),
                preferred_element_type=F32,
            )
            total = term if total is None else total + term
        acc[4 * group + s] = total

    for m in range(3):
        net.wait(xg.at[twin[2], spans[m]], g_in.at[m, twin[2]], twin)
    relay = core == z // 2

    def relay_share(o):
        s = (b + o) % blocks
        for row in range(n_dp):
            block, ok = xb.at[chip, s, pl.ds(0, SHARE[row])], relay & (y == row)
            net.wait(block, b_in.at[chip, s], across, ok)
            net.go(block, block, b_in.at[chip, s], far, ok)
            net.go(block, block, b_in.at[chip, s], twin, ok)

    for s in range(4):
        for group in range(2):
            forward_part(chip, range(8), group, s, True)
    early, late = range(EARLY), range(EARLY, 8)
    other = 2 * (1 - chip) + 1 - core

    def far_arrived(m):
        net.wait(xg.at[cf, spans[m]], g_in.at[m, cf], far)
        net.go(xg.at[cf, spans[m]], xg.at[cf, spans[m]], g_in.at[m, cf], twin)

    def far_passed(m):
        net.wait(xg.at[other, spans[m]], g_in.at[m, other], twin)

    far_arrived(0)
    far_passed(0)
    for s in range(4):
        forward_part(1 - chip, early, 0, s, False)
    ahead = acc[0]
    for s in (1, 2, 3):
        ahead = ahead + forward_shift(acc[s], s)
    carry[0] = ahead
    net.go(carry.at[0], carry.at[1], misc_in.at[1], right, z < n_space - 1)
    row_start(x8.at[c, b], e_in.at[b])
    for s in range(4):
        forward_part(1 - chip, early, 1, s, False)
    far_arrived(1)
    far_arrived(2)
    far_passed(1)
    far_passed(2)

    for s in range(4):
        forward_part(1 - chip, late, 1, s, False)
    for o in range(1, blocks):
        relay_share(o)
    diagonal = lax.broadcasted_iota(jnp.int32, (part, part), 0) == lax.broadcasted_iota(jnp.int32, (part, part), 1)
    u = jnp.sum(jnp.where(diagonal, b_ref[...], 0.0), axis=1, keepdims=True) + acc[4]
    for s in (1, 2, 3):
        u = u + forward_shift(acc[4 + s], s)

    @pl.when(z == 0)
    def _():
        carry[1] = jnp.zeros_like(carry[1])

    net.wait(carry.at[1], misc_in.at[1], left, z > 0)
    u = u + carry[1]
    k0 = 0.7978845608028654
    th = jnp.tanh(k0 * (u + 0.044715 * (u * u * u)))
    slope = 0.5 * (1.0 + th) + 0.5 * u * (1.0 - th * th) * k0 * (1.0 + 3 * 0.044715 * u * u)
    dysh[0, b] = (g_ref[...].astype(F32) * slope).astype(BF)
    act_ref[...] = (0.5 * u * (1.0 + th)).astype(BF)

    def dy_of(s):
        return dysh.at[0, s]

    def dy_sem(s):
        return dy_in.at[s]

    row_start(dysh.at[0, b], dy_in.at[b])
    net.go(dysh.at[0, b], dyt.at[0, 0], dyt_in.at[0], twin)
    own_slots = []
    for hx in range(2):
        own_slots.append(
            pltpu.make_async_copy(
                xg.at[2 * hx + z // 2, pl.ds(4 * y, 4), pl.ds(pl.multiple_of(rows * (z % 2), rows), rows)],
                xb.at[hx, b],
                local_sem.at[1 + hx],
            )
        )
        own_slots[-1].start()

    def shift_slot(s):
        wide = dysh[0, s].astype(F32)
        for k in (1, 2, 3):
            dysh[k, s] = backward_shift(wide, k).astype(BF)

    for k in range(3):
        row_step(k, eight, eight_sem)
    shift_slot(b)
    for k in range(3):
        row_step(k, dy_of, dy_sem)
    nxt = y * n_space + jnp.minimum(z + 1, n_space - 1)
    net.go(dysh.at[0, nxt], dyt.at[0, 1], dyt_in.at[1], twin, z < n_space - 1)
    for o in range(1, n_space):
        shift_slot(y * n_space + (z + o) % n_space)
    for zz in range(n_space):
        chain_end(zz, eight, eight_sem)

    for r in range(n_dp):
        mine = x8.at[c, pl.ds(n_space * r, n_space)]
        net.go(mine, mine, e_all.at[r, c], far)
        net.go(mine, mine, e_all.at[r, c], twin)
    for zz in (z, *nearest):
        chain_end(zz, dy_of, dy_sem, shift_slot)

    for o in range(1, blocks):
        s = (b + o) % blocks
        for row in range(n_dp):
            net.wait(
                xb.at[chip, s, pl.ds(0, SHARE[row])], b_in.at[chip, s], twin, jnp.logical_not(relay) & (y == row)
            )
    for copy in own_slots:
        copy.wait()

    def share_half(row, i, side):
        _, (k1, k2, k3), k = share_taps(row)[i]
        total = None
        for v in range(n_dp):
            for zz in range(n_space - (k1 == 0)):
                s = v * n_space + zz
                term = lax.dot_general(
                    dysh[shift_of(k2, k3), s + (k1 == 0)], xb[side, s, k], NT, preferred_element_type=F32
                )
                total = term if total is None else total + term
        return total * scale

    def share_piece(row, i, side):
        first = 2 * (i % (PIECES // 2))
        low = share_half(row, first, side)
        high = share_half(row, first + 1, side) if first + 1 < len(share_taps(row)) else jnp.zeros_like(low)
        dwb_ref[b, i] = jnp.concatenate([low, high], axis=1).astype(BF)

    def dw_of(m):
        lo, hi = CHUNKS[m]
        return lambda s: dwb_ref.at[s, pl.ds(lo, hi - lo)]

    def dw_sem(m):
        return lambda s: dw_in.at[m, s]

    def share_chunk(m):
        lo, hi = CHUNKS[m]
        for row in range(n_dp):
            @pl.when(y == row)
            def _():
                for i in range(lo, hi):
                    share_piece(row, i, chip if i < PIECES // 2 else 1 - chip)
        chain_start(dw_of(m)(b), dw_sem(m)(b))

    for m in (0, 1):
        share_chunk(m)
    for o in range(1, blocks):
        s = (b + o) % blocks
        for row in range(n_dp):
            other_half, ok = xb.at[1 - chip, s, pl.ds(0, SHARE[row])], relay & (y == row)
            net.wait(other_half, b_in.at[1 - chip, s], far, ok)
            net.go(other_half, other_half, b_in.at[1 - chip, s], twin, ok)
    for o in range(1, blocks):
        s = (b + o) % blocks
        for row in range(n_dp):
            net.wait(
                xb.at[1 - chip, s, pl.ds(0, SHARE[row])], b_in.at[1 - chip, s], twin,
                jnp.logical_not(relay) & (y == row),
            )
    for m in (2, 3):
        share_chunk(m)

    @pl.when(z == n_space - 1)
    def _():
        dyt[0, 1] = jnp.zeros_like(dyt[0, 1])

    net.wait(dyt.at[0, 0], dyt_in.at[0], twin)
    net.wait(dyt.at[0, 1], dyt_in.at[1], twin, z < n_space - 1)
    for i in range(2):
        wide = dyt[0, i].astype(F32)
        for k in (1, 2, 3):
            dyt[k, i] = backward_shift(wide, k).astype(BF)
    net.wait(w2.at[1], misc_in.at[0], twin)
    edge = jnp.where(z < n_space - 1, 1.0, 0.0).astype(BF)

    def input_grad(j, p, ph):
        total = None
        for t, (k1, k2, k3) in enumerate(TAPS):
            if phase_of(k2, k3) != ph or (k1 != 1) != (p == 1):
                continue
            s = shift_of(k2, k3)
            here = dysh[s, nxt] * edge if k1 == 0 else dysh[s, b]
            for i, view in enumerate((here, dyt[s, int(k1 == 0)])):
                term = lax.dot_general(
                    w2[i, :, columns(t, j, 1)], view, TN, preferred_element_type=F32
                )
                total = term if total is None else total + term
        return total

    for p in range(2):
        for ph in range(4):
            gx_far[p, ph] = input_grad(cf, p, ph).astype(BF)
        net.go(gx_far.at[p], gx_in.at[p], gx_sem.at[p], far)

    def pass_on(d, *chunks):
        for m in chunks:
            chain_step(d, dw_of(m), dw_sem(m))

    pass_on(1, 0, 1)
    for ph in range(4):
        gx_own[0, ph] = input_grad(c, 0, ph)
    pass_on(1, 2, 3)
    for ph in range(4):
        gx_own[1, ph] = input_grad(c, 1, ph)
    pass_on(2, 0, 1)

    for r in range(n_dp):
        theirs = x8.at[cf, pl.ds(n_space * r, n_space)]
        net.wait(theirs, e_all.at[r, cf], far)
        net.go(theirs, theirs, e_all.at[r, cf], twin)
    pass_on(2, 2, 3)
    for r in range(n_dp):
        for j in (twin[2], other):
            net.wait(x8.at[j, pl.ds(n_space * r, n_space)], e_all.at[r, j], twin)
    for k in range(2):
        for v in range(n_dp):
            for zz in range(n_space - (k == 0)):
                s = v * n_space + zz
                term = lax.dot_general(
                    dysh[:, s + (k == 0)].reshape(4 * part, CELLS),
                    x8[:, s].reshape(n_chan * part, CELLS),
                    NT,
                    preferred_element_type=F32,
                ) * scale
                if s == 0:
                    d8_ref[k] = term
                else:
                    d8_ref[k] += term
        pass_on(3, *((0, 1) if k == 0 else (2, 3)))
    ones = jnp.ones((8, CELLS), BF)
    total = None
    for s in range(blocks):
        term = lax.dot_general(ones, dysh[0, s], NT, preferred_element_type=F32)
        total = term if total is None else total + term
    db_ref[...] = total * scale

    for p in range(2):
        net.wait(gx_in.at[p], gx_sem.at[p], far)
    for p in range(2):
        cells = [(gx_own[p, ph] + gx_in[p, ph].astype(F32)).astype(BF) for ph in range(4)]
        for h in range(2):
            strip = jnp.concatenate([cell[:, h * half : (h + 1) * half] for cell in cells], axis=1)
            gx_ref[p, :, 2 * CELLS * h : 2 * CELLS * (h + 1)] = lax.dot_general(
                strip, parity_block(), NT, preferred_element_type=F32
            ).astype(BF)
    for m in range(len(CHUNKS)):
        for zz in range(n_space):
            chain_end(zz, dw_of(m), dw_sem(m))
    net.drain()


def finish_kernel(n_space, part, dwb_ref, d8_ref, gx_ref, act_ref, db_ref, act_out, gx_out, dw_out, db_out, wide, sem):
    chip = lax.axis_index("chan") // 2
    copies = [
        pltpu.make_async_copy(gx_ref, gx_out, sem.at[len(TAPS)]),
        pltpu.make_async_copy(act_ref, act_out, sem.at[len(TAPS) + 1]),
    ]
    for copy in copies:
        copy.start()
    db_out[...] = db_ref[0:1]
    width = 4 * part
    where = {}
    for row in range(2):
        for i, (t, _, _) in enumerate(share_taps(row)):
            where[t] = (row, i)
    low = lax.broadcasted_iota(jnp.int32, (part, part), 1) < part // 2
    for t in sorted(range(len(TAPS)), key=lambda t: t in where):
        k1, k2, k3 = TAPS[t]
        first = t * width
        if t in where:
            row, i = where[t]
            for j in range(4):
                q = i // 2 + PIECES // 2 * jnp.where(chip == j // 2, 0, 1)
                even = dwb_ref[row * n_space + 2 * (j % 2), q].astype(F32)
                odd = dwb_ref[row * n_space + 2 * (j % 2) + 1, q].astype(F32)
                if i % 2:
                    even = pltpu.roll(even, part // 2, 1)
                else:
                    odd = pltpu.roll(odd, part // 2, 1)
                wide[:, first + j * part : first + (j + 1) * part] = jnp.where(low, even, odd)
        else:
            s = shift_of(k2, k3)
            wide[:, first : first + width] = d8_ref[int(k1 == 2), s * part : (s + 1) * part]
        span = pl.ds(first, width)
        copies.append(pltpu.make_async_copy(wide.at[:, span], dw_out.at[:, span], sem.at[t]))
        copies[-1].start()
    for copy in copies:
        copy.wait()


def per_device_shared(volumes, kernel, bias, act_grad):
    batch, planes, part, cells = volumes.shape
    filters = kernel.shape[0]
    width = kernel.shape[1] // 27
    sizes = tuple(lax.axis_size(a) for a in ("dp", "space", "chan"))
    n_dp, n_space, n_chan = sizes
    blocks = n_dp * n_space
    dma = pltpu.SemaphoreType.DMA
    flops = 2 * 27 * width * filters * CELLS
    ANY = pl.BlockSpec(memory_space=pl.ANY)
    act, gx, dwb, d8, db = pl.pallas_call(
        functools.partial(layer_kernel, sizes, width, 1.0 / (batch * n_dp)),
        out_shape=(
            shape(filters, CELLS),
            shape(planes, part, cells),
            shape(blocks, PIECES, filters, part),
            shape(2, 4 * filters, width, dtype=F32),
            shape(8, filters, dtype=F32),
        ),
        in_specs=[ANY] * 4,
        out_specs=[VM] * 5,
        scratch_shapes=(
            pltpu.VMEM((planes, part, cells), BF),
            pltpu.VMEM((filters, CELLS), BF),
            pltpu.VMEM((1, filters), F32),
            pltpu.VMEM((2, filters, 27 * width), BF),
            pltpu.VMEM((n_chan, 8, part, CELLS), BF),
            pltpu.VMEM((2, blocks, 4, part // 2, CELLS), BF),
            pltpu.VMEM((n_chan, blocks, part, CELLS), BF),
            pltpu.VMEM((8, filters, CELLS), F32),
            pltpu.VMEM((2, filters, CELLS), F32),
            pltpu.VMEM((4, blocks, filters, CELLS), BF),
            pltpu.VMEM((4, 2, filters, CELLS), BF),
            pltpu.VMEM((2, 4, part, CELLS), BF),
            pltpu.VMEM((2, 4, part, CELLS), BF),
            pltpu.VMEM((2, 4, part, CELLS), F32),
            dma((SENDS,)),
            dma((6,)),
            dma((3, n_chan)),
            dma((2, blocks)),
            dma((blocks,)),
            dma((n_dp, n_chan)),
            dma((blocks,)),
            dma((2,)),
            dma((len(CHUNKS), blocks)),
            dma((2,)),
            dma((2,)),
        ),
        compiler_params=pltpu.CompilerParams(
            vmem_limit_bytes=46 << 20, collective_id=0, has_side_effects=True
        ),
        cost_estimate=pl.CostEstimate(flops=5 * flops, bytes_accessed=12 << 20, transcendentals=0),
    )(
        *(
            pltpu.with_memory_space_constraint(array, pltpu.HBM)
            for array in (
                volumes.reshape(planes, part, cells),
                kernel,
                bias.reshape(1, filters),
                act_grad.reshape(filters, CELLS),
            )
        )
    )
    act, gx, dw, db = pl.pallas_call(
        functools.partial(finish_kernel, n_space, part),
        out_shape=(
            shape(filters, CELLS),
            shape(planes, part, cells),
            shape(filters, 27 * width, dtype=F32),
            shape(1, filters, dtype=F32),
        ),
        in_specs=[VM] * 5,
        out_specs=[ANY, ANY, ANY, VM],
        scratch_shapes=(pltpu.VMEM((filters, 27 * width), F32), dma((len(TAPS) + 2,))),
        compiler_params=pltpu.CompilerParams(vmem_limit_bytes=40 << 20),
        cost_estimate=pl.CostEstimate(flops=0, bytes_accessed=12 << 20, transcendentals=0),
    )(dwb, d8, gx, act, db)
    return act.reshape(act_grad.shape), gx.reshape(volumes.shape), dw, db.reshape(filters)


def solution(mesh):
    shared = (mesh.shape["dp"], mesh.shape["space"], mesh.shape["chan"]) == (2, 4, 4)
    in_specs = (
        P("dp", "space", "chan", None),
        P("chan", None),
        P("chan"),
        P("dp", "space", "chan", None),
    )
    out_specs = (
        P("dp", "space", "chan", None),
        P("dp", "space", "chan", None),
        P("chan", None),
        P("chan"),
    )
    return jax.shard_map(
        per_device_shared if shared else per_device,
        mesh=mesh, in_specs=in_specs, out_specs=out_specs, check_vma=False,
    )
```
